128 devices in a mesh: gx: 16 (over z, x), gy: 8 (over y, core).
Axes of the slice: x: 4, y: 4, z: 4, core: 2. Of those that a mesh axis runs over, the one named last changes fastest.
Arguments:
- velocity: bfloat16 [3, 16, 2048, 2048], P(None, None, 'gx', 'gy'), may hold values from -4 to 4
- kinetic_energy: bfloat16 [16, 2048, 2048], P(None, 'gx', 'gy'), may hold values from 0.019897461 to 0.3984375
- dissipation_rate: bfloat16 [16, 2048, 2048], P(None, 'gx', 'gy'), may hold values from 1 to 8
- adjoint_start: float32 [3, 16, 2048, 2048], P(None, None, 'gx', 'gy'), may hold values from -6 to 6
- interp_weight: bfloat16 [128, 256], replicated, may hold values from -0.375 to 0.375
- observed: float32 [3, 32768, 128], P(None, ('gx', 'gy')), may hold values from -6 to 6
- window_weight: float32 [32768], P(('gx', 'gy')), may hold values from 0.5 to 2
- window_source: int32 [32768, 1], P(('gx', 'gy')), may hold values from 0 to 127; in each aligned block of 256 rows (0 to 255, 256 to 511, ...) at most 4 rows name the same one
- window_block: int32 [32768], P(('gx', 'gy')), may hold values from 0 to 2047
- window_count: int32 [32768], P(('gx', 'gy')), may hold values from 1 to 256
Outputs:
- adjoint_end: float32 [3, 16, 2048, 2048], P(None, None, 'gx', 'gy')
The draws below stay inside these ranges and needn't reach their ends.
Inputs may be any that keep to these rules, and one draw needn't show every extreme that they name: `window_source`: among the windows of one owner device (aligned blocks of 256 rows), at most 4 name the same source device, a bound that some block reaches.
All inputs are finite; a program needn't handle non-finite values.
Results may differ from the reference program's by a relative error of at most 0.00072.
Values may be sent and summed in bfloat16 or wider, within the bound.
A program may use at most 192 MiB of HBM per device.

```python
import math
import jax
import jax.numpy as jnp
import numpy as np
from jax import lax

CX = 128
CY = 256
NZ = 16
LINE = 256
M = 128
W_DEV = 256
SWEEPS = 2
NX = 2048
NY = 2048
W_ALL = 32768
BLK_DEV = 2048
CAP = 4
N_GX = 16
N_GY = 8
DEVICES = 128


def set_ends(result, rng, smallest, top_value):
    longest = result.shape.index(max(result.shape))
    spots = []
    for shift in (0, 1):
        where = [jax.random.randint(jax.random.fold_in(rng, axis), (), 0, length) for axis, length in enumerate(result.shape)]
        where[longest] = (where[longest] + shift) % result.shape[longest]
        spots.append(tuple(where))
    return result.at[spots[0]].set(smallest).at[spots[1]].set(top_value)


def block_levels(own_key, extent, shards, least, top_value):
    level = 1.0
    for axis_at, blocks in shards:
        steps = jax.random.uniform(jax.random.fold_in(jax.random.fold_in(own_key, 6), axis_at), (blocks,), jnp.float32, least / len(shards), top_value / len(shards))
        level = level * jnp.repeat(jnp.exp(steps), extent[axis_at] // blocks).reshape((-1,) + (1,) * (len(extent) - 1 - axis_at))
    return level


def routed_block(own_key, own, number, rows, count, top, reach, slope):
    order = jax.random.permutation(own_key, count)
    crowded, ordinary = portions_of(count, rows * top, reach, slope, True), portions_of(count, rows * top, reach, slope, False)
    places = jnp.arange(count)

    def named(sizes, turn):
        used = int((sizes > 0).sum())
        fixed = max(1, used // 4)
        passed = fixed + (places - fixed + turn * (used - fixed)) % max(1, count - fixed)
        return jnp.zeros((count,), jnp.int32).at[order[jnp.where(places < fixed, places, passed)]].set(jnp.asarray(sizes, jnp.int32))

    sizes = jnp.where(number % 4 == 0, named(crowded, number // 4), named(ordinary, number - number // 4 - 1))
    mixed = jax.random.permutation(jax.random.fold_in(own, 3), count)
    donor, receiver = mixed[0:count // 2 * 2:2], mixed[1:count // 2 * 2:2]
    slack = jnp.minimum(sizes[donor] - 1, reach - sizes[receiver]) // 2
    slack = jnp.where((donor == order[0]) | (receiver == order[0]) | (sizes[receiver] == 0), 0, jnp.maximum(slack, 0))
    passed = jax.random.randint(jax.random.fold_in(own, 4), (count // 2,), 0, 1 << 20) % (slack + 1)
    sizes = sizes.at[donor].add(-passed).at[receiver].add(passed)
    items = jnp.searchsorted(jnp.cumsum(sizes), jnp.arange(rows * top), side="right").astype(jnp.int32)
    table = items.reshape(top, rows).T
    table = table[jax.random.permutation(jax.random.fold_in(own, 1), rows)]
    turn = jax.random.randint(jax.random.fold_in(own, 2), (rows, 1), 0, top)
    return jnp.take_along_axis(table, (jnp.arange(top)[None, :] + turn) % top, axis=1)


def portions_of(amount, total, bound, skew, full):
    loads = [(1 << 20) // math.isqrt(grade ** skew) + 1 for grade in range(1, amount + 1)]
    largest = bound if full else min(bound, max(-(-total // amount), total * loads[0] // sum(loads)))
    least = 1 if total - largest >= amount - 1 else 0
    given, spare = [largest] + [least] * (amount - 1), total - largest - least * (amount - 1)
    while spare > 0:
        candidates = [i for i in range(1, amount) if given[i] < largest] or [i for i in range(1, amount) if given[i] < bound]
        mass, remaining = sum([loads[i] for i in candidates]), spare
        for i in candidates:
            more = min(bound - given[i], max(1, remaining * loads[i] // mass), spare)
            given[i] = given[i] + more
            spare = spare - more
    return np.array(given)


def bell_draw(rng, dims, deviation, limit, shards=(), kind=jnp.bfloat16):
    gain = block_levels(rng, dims, shards, -0.22, 0.18) if shards else 1.0
    entries = jax.random.normal(rng, dims, jnp.float32) * deviation * gain
    return jnp.minimum(jnp.maximum(entries, -limit), limit).astype(kind)


def setup_inputs(seed: int = 0) -> dict:
    keys = jax.random.split(jax.random.key(seed), 11)
    velocity = bell_draw(keys[0], (3, NZ, NX, NY), 1.0, 4.0, ((2, 16), (3, 8)))
    kinetic_energy = jnp.clip(jnp.exp(math.log(0.3984375) - 2.9969585 * jax.random.uniform(keys[1], (NZ, NX, NY), jnp.float32) ** block_levels(keys[1], (NZ, NX, NY), ((1, 16), (2, 8)), -0.2, 0.2)), 0.019897461, 0.3984375).astype(jnp.bfloat16)
    dissipation_rate = jnp.clip(jnp.exp(math.log(8.0) - 2.0794415 * jax.random.uniform(keys[2], (NZ, NX, NY), jnp.float32) ** block_levels(keys[2], (NZ, NX, NY), ((1, 16), (2, 8)), -0.2, 0.2)), 1.0, 8.0).astype(jnp.bfloat16)
    adjoint_start = bell_draw(keys[3], (3, NZ, NX, NY), 1.0, 6.0, ((2, 16), (3, 8)), jnp.float32)
    interp_weight = bell_draw(keys[4], (M, LINE), LINE ** -0.5, 0.375)
    observed = bell_draw(keys[5], (3, W_ALL, M), 1.0, 6.0, ((1, 128),), jnp.float32)
    window_weight = jnp.clip(jnp.exp(math.log(2.0) - 1.3862944 * jax.random.uniform(keys[6], (W_ALL,), jnp.float32) ** block_levels(keys[6], (W_ALL,), ((0, 128),), -0.2, 0.2)), 0.5, 2.0)
    window_source_keys = jax.random.split(jax.random.fold_in(keys[7], 1), W_ALL // W_DEV)
    window_source_turns = jax.random.permutation(jax.random.fold_in(keys[7], 3), W_ALL // W_DEV)
    window_source = jax.vmap(lambda own, number: routed_block(jax.random.fold_in(keys[7], 2), own, number, W_DEV, DEVICES, 1, CAP, 2))(window_source_keys, window_source_turns).reshape((W_ALL, 1))
    window_block = set_ends(jax.random.randint(keys[8], (W_ALL,), 0, BLK_DEV), jax.random.fold_in(keys[8], 1), 0, BLK_DEV - 1).astype(jnp.int32)
    window_count = set_ends(jax.random.randint(keys[9], (W_ALL,), 1, LINE + 1), jax.random.fold_in(keys[9], 1), 1, LINE).astype(jnp.int32)
    return dict(velocity=velocity, kinetic_energy=kinetic_energy, dissipation_rate=dissipation_rate, adjoint_start=adjoint_start, interp_weight=interp_weight, observed=observed, window_weight=window_weight, window_source=window_source, window_block=window_block, window_count=window_count)


base_viscosity = 0.05
pseudo_step = 0.4


def part(field, step_z, step_x, step_y):
    size_z = field.shape[1] - 2
    size_x = field.shape[2] - 2
    size_y = field.shape[3] - 2
    return field[:, 1 + step_z:1 + step_z + size_z, 1 + step_x:1 + step_x + size_x, 1 + step_y:1 + step_y + size_y]


def transport(adjoint_pad, state_pad, forcing):
    zpad = ((0, 0), (1, 1), (0, 0), (0, 0))
    adjoint = jnp.pad(adjoint_pad, zpad)
    states = jnp.pad(state_pad.astype(jnp.float32), zpad)
    viscous = states[3:4]
    centre = part(adjoint, 0, 0, 0)
    visc_centre = part(viscous, 0, 0, 0)
    summed = forcing
    for component, shift in ((0, (0, 1, 0)), (1, (0, 0, 1)), (2, (1, 0, 0))):
        step_z, step_x, step_y = shift
        speed = states[component:component + 1]
        upper = part(adjoint, step_z, step_x, step_y)
        lower = part(adjoint, -step_z, -step_x, -step_y)
        speed_up = part(speed, step_z, step_x, step_y)
        speed_down = part(speed, -step_z, -step_x, -step_y)
        visc_up = part(viscous, step_z, step_x, step_y)
        visc_down = part(viscous, -step_z, -step_x, -step_y)
        summed = summed + 0.5 * (speed_down * lower - speed_up * upper)
        summed = summed + 0.5 * (visc_up + visc_centre) * (upper - centre) - 0.5 * (visc_centre + visc_down) * (centre - lower)
    return centre + pseudo_step * summed


def reference(velocity, kinetic_energy, dissipation_rate, adjoint_start, interp_weight, observed, window_weight, window_source, window_block, window_count):
    viscosity = (base_viscosity + kinetic_energy.astype(jnp.float32) / dissipation_rate.astype(jnp.float32)).astype(jnp.bfloat16)
    states = jnp.concatenate([velocity, viscosity[None]], 0)
    state_pad = jnp.pad(states, ((0, 0), (0, 0), (1, 1), (1, 1)))
    lines = velocity.reshape(3, NZ, N_GX, CX, N_GY, CY // LINE, LINE).transpose(0, 2, 4, 1, 3, 5, 6).reshape(3, N_GX * N_GY * BLK_DEV, LINE)
    global_index = (window_source[:, 0] * BLK_DEV + window_block).astype(jnp.int32)
    cells = jnp.arange(LINE, dtype=jnp.int32)
    inside = (cells[None, :] < window_count[:, None]).astype(jnp.float32)
    masked = lines[:, global_index].astype(jnp.float32) * inside[None]
    weights = interp_weight.astype(jnp.float32)
    predicted = jnp.einsum("cwj,mj->cwm", masked, weights)
    residual = window_weight[None, :, None] * (predicted - observed)
    line_forcing = inside[None] * jnp.einsum("cwm,mj->cwj", residual, weights, precision=lax.Precision.HIGHEST)
    placed = jnp.zeros((3, N_GX * N_GY * BLK_DEV, LINE), jnp.float32).at[:, global_index].add(line_forcing)
    forcing = placed.reshape(3, N_GX, N_GY, NZ, CX, CY // LINE, LINE).transpose(0, 3, 1, 4, 2, 5, 6).reshape(3, NZ, NX, NY)
    adjoint = adjoint_start
    for sweep in range(SWEEPS):
        adjoint = transport(jnp.pad(adjoint, ((0, 0), (0, 0), (1, 1), (1, 1))), state_pad, forcing)
    return adjoint
```

```python
import functools

import jax
import jax.numpy as jnp
from jax import lax
from jax.experimental import pallas as pl
from jax.experimental.pallas import tpu as pltpu
from jax.sharding import PartitionSpec as P

MESH = pl.DeviceIdType.MESH
SWEEPS = 2
CAP = 4
LANES = 128
SUB = 8

base_viscosity = 0.05
pseudo_step = 0.4
half_step = 0.5 * pseudo_step

META = 385
PAD = 8


def lane_iota(rows=SUB):
    return lax.broadcasted_iota(jnp.int32, (rows, LANES), 1)


def split(x, pieces):
    out = []
    for _ in range(pieces):
        piece = x.astype(jnp.bfloat16)
        out.append(piece)
        x = x - piece.astype(jnp.float32)
    return out


def put_row(ref, side, number, row, lanes=slice(None)):
    base = pl.multiple_of(number // SUB * SUB, SUB)
    old = ref[side, pl.ds(base, SUB), lanes]
    here = lax.broadcasted_iota(jnp.int32, old.shape, 0) == number - base
    ref[side, pl.ds(base, SUB), lanes] = jnp.where(here, jnp.broadcast_to(row, old.shape), old)


def fill_slots(meta_ref, obs_ref, slots_ref, peers):
    windows = meta_ref.shape[1]
    meta = meta_ref[...]
    source_row = meta[0:1]
    columns = jnp.concatenate(
        [meta, jnp.zeros((LANES - meta.shape[0], windows), jnp.float32)], axis=0
    ).T
    source_col = columns[:, 0:1]
    first = lax.broadcasted_iota(jnp.int32, (windows, windows), 0)
    second = lax.broadcasted_iota(jnp.int32, (windows, windows), 1)
    same = (source_col == source_row) & (first < second)
    place = jnp.sum(same.astype(jnp.float32), axis=0, keepdims=True)
    slot = (source_row * CAP + place).astype(jnp.int32)
    slots = peers * CAP
    chosen = (lax.broadcasted_iota(jnp.int32, (slots, windows), 0) == slot).astype(jnp.bfloat16)
    for part in range(4):
        values = columns if part == 3 else obs_ref[part]
        total = jnp.zeros((slots, LANES), jnp.float32)
        for piece in reversed(split(values, 3)):
            total = total + jnp.dot(chosen, piece, preferred_element_type=jnp.float32)
        slots_ref[:, part * LANES : (part + 1) * LANES] = total


def prep_kernel(meta_ref, obs_ref, ux_ref, uy_ref, ke_ref, dr_ref, a_ref, slots_ref, visc_ref, xe_ref, ye_ref):
    z = pl.program_id(0)
    planes = pl.num_programs(0)
    rows, cols = ke_ref.shape[1:]

    @pl.when(z == 0)
    def _():
        fill_slots(meta_ref, obs_ref, slots_ref, slots_ref.shape[0] // CAP)

    visc = (
        base_viscosity + ke_ref[0].astype(jnp.float32) / dr_ref[0].astype(jnp.float32)
    ).astype(jnp.bfloat16)
    visc_ref[0] = visc
    fields = [a_ref[c, 0] for c in range(3)]
    @pl.when(z == 0)
    def _():
        xe_ref[...] = jnp.zeros_like(xe_ref)
        ye_ref[...] = jnp.zeros_like(ye_ref)

    for side, at in ((0, 0), (1, rows - 1)):
        for c in range(3):
            put_row(xe_ref, side, c * planes + z, fields[c][at : at + 1])
        put_row(xe_ref, side, 3 * planes + z, ux_ref[0, 0].astype(jnp.float32)[at : at + 1])
        put_row(xe_ref, side, 4 * planes + z, visc.astype(jnp.float32)[at : at + 1])
    fields = fields + [uy_ref[0, 0].astype(jnp.float32), visc.astype(jnp.float32)]
    lanes = lane_iota(rows)
    for side in range(2):
        total = ye_ref[side]
        for k, field in enumerate(fields):
            part = field[:, :LANES] if side == 0 else field[:, cols - LANES :]
            lane = k * planes + z
            moved = pltpu.roll(part, lane if side == 0 else lane + 1, axis=1)
            total = jnp.where(lanes == lane, moved, total)
        ye_ref[side] = total


def prep(meta, observed, velocity, kinetic_energy, dissipation_rate, adjoint, peers):
    planes, rows, cols = kinetic_energy.shape
    windows = meta.shape[1]
    plane = pl.BlockSpec((1, rows, cols), lambda z: (z, 0, 0))
    return pl.pallas_call(
        prep_kernel,
        name="prep",
        grid=(planes,),
        in_specs=[
            pl.BlockSpec((8, windows), lambda z: (0, 0)),
            pl.BlockSpec((3, windows, LANES), lambda z: (0, 0, 0)),
            pl.BlockSpec((1, 1, rows, cols), lambda z: (0, z, 0, 0)),
            pl.BlockSpec((1, 1, rows, cols), lambda z: (1, z, 0, 0)),
            plane,
            plane,
            pl.BlockSpec((3, 1, rows, cols), lambda z: (0, z, 0, 0)),
        ],
        out_specs=[
            pl.BlockSpec((peers * CAP, 4 * LANES), lambda z: (0, 0)),
            plane,
            pl.BlockSpec((2, 5 * planes, cols), lambda z: (0, 0, 0)),
            pl.BlockSpec((2, rows, LANES), lambda z: (0, 0, 0)),
        ],
        out_shape=[
            jax.ShapeDtypeStruct((peers * CAP, 4 * LANES), jnp.float32),
            jax.ShapeDtypeStruct((planes, rows, cols), jnp.bfloat16),
            jax.ShapeDtypeStruct((2, 5 * planes, cols), jnp.float32),
            jax.ShapeDtypeStruct((2, rows, LANES), jnp.float32),
        ],
        compiler_params=pltpu.CompilerParams(vmem_limit_bytes=32 << 20),
    )(meta, observed, velocity, velocity, kinetic_energy, dissipation_rate, adjoint)


def exchange_kernel(n_gx, n_gy, with_slots, *refs):
    if with_slots:
        s_ref, xe_ref, ye_ref, r_ref, xh_ref, yh_ref, send, recv, all_send, all_recv, local = refs
    else:
        xe_ref, ye_ref, xh_ref, yh_ref, send, recv = refs
    gx, gy = lax.axis_index("gx"), lax.axis_index("gy")
    me = gx * n_gy + gy
    peers = n_gx * n_gy

    def device(step):
        peer = lax.rem(me + step, peers)
        return peer, (peer // n_gy, lax.rem(peer, n_gy))

    lower_x = (lax.rem(gx + n_gx - 1, n_gx), gy)
    upper_x = (lax.rem(gx + 1, n_gx), gy)
    lower_y = (gx, lax.rem(gy + n_gy - 1, n_gy))
    upper_y = (gx, lax.rem(gy + 1, n_gy))
    sides = (
        (xe_ref.at[1], xh_ref.at[0], upper_x),
        (xe_ref.at[0], xh_ref.at[1], lower_x),
        (ye_ref.at[1], yh_ref.at[0], upper_y),
        (ye_ref.at[0], yh_ref.at[1], lower_y),
    )
    barrier = pltpu.get_barrier_semaphore()
    if with_slots:

        @pl.loop(1, peers)
        def _(step):
            pl.semaphore_signal(barrier, inc=1, device_id=device(step)[1], device_id_type=MESH)

        pl.semaphore_wait(barrier, peers - 1)
    else:
        for _, _, where in sides:
            pl.semaphore_signal(barrier, inc=1, device_id=where, device_id_type=MESH)
        pl.semaphore_wait(barrier, 4)
    copies = []
    for k, (source, target, where) in enumerate(sides):
        copy = pltpu.make_async_remote_copy(
            source, target, send.at[k], recv.at[k], device_id=where, device_id_type=MESH
        )
        copy.start()
        copies.append(copy)
    if with_slots:
        own = pltpu.make_async_copy(s_ref.at[me], r_ref.at[me], local)
        own.start()

        @pl.loop(1, peers)
        def _(step):
            peer, where = device(step)
            pltpu.make_async_remote_copy(
                s_ref.at[peer], r_ref.at[me], all_send, all_recv, device_id=where, device_id_type=MESH
            ).start()

        own.wait()
        rest = pl.ds(0, peers - 1)
        pltpu.make_async_copy(s_ref.at[rest], s_ref.at[rest], all_send).wait()
        pltpu.make_async_copy(r_ref.at[rest], r_ref.at[rest], all_recv).wait()
    for copy in copies:
        copy.wait()


def exchange(xe, ye, slots, n_gx, n_gy, collective_id):
    arrays = ([slots] if slots is not None else []) + [xe, ye]
    dma = pltpu.SemaphoreType.DMA
    scratch = [dma((4,)), dma((4,))] + ([dma, dma, dma] if slots is not None else [])
    any_space = pl.BlockSpec(memory_space=pl.ANY)
    return pl.pallas_call(
        functools.partial(exchange_kernel, n_gx, n_gy, slots is not None),
        name="exchange_slots" if slots is not None else "exchange_edges",
        in_specs=[any_space] * len(arrays),
        out_specs=[any_space] * len(arrays),
        out_shape=[jax.ShapeDtypeStruct(a.shape, a.dtype) for a in arrays],
        scratch_shapes=scratch,
        compiler_params=pltpu.CompilerParams(collective_id=collective_id, has_side_effects=True),
    )(*arrays)


def line_forcing(recv_ref, vel_ref, weight_ref, high_ref, low_ref):
    slots = recv_ref.shape[0]
    planes, rows, cols = vel_ref.shape[1:]
    weights = weight_ref[...]
    block = recv_ref[:, META : META + 1].astype(jnp.int32)
    count = recv_ref[:, META + 1 : META + 2].astype(jnp.int32)
    scale = recv_ref[:, META + 2 : META + 3]
    inside = lax.broadcasted_iota(jnp.int32, (slots, cols), 1) < count
    group = 4
    lines = [jnp.zeros((slots, cols), jnp.float32) for _ in range(3)]
    for q in range(planes // group):
        number = lax.broadcasted_iota(jnp.int32, (slots, group * rows), 1) + q * group * rows
        chosen = (number == block).astype(jnp.bfloat16)
        for c in range(3):
            some = vel_ref[c, q * group : (q + 1) * group].reshape(group * rows, cols)
            lines[c] = lines[c] + jnp.dot(chosen, some, preferred_element_type=jnp.float32)
    for c in range(3):
        masked = jnp.where(inside, lines[c], 0.0).astype(jnp.bfloat16)
        predicted = lax.dot_general(
            masked, weights, (((1,), (1,)), ((), ())), preferred_element_type=jnp.float32
        )
        residual = scale * (predicted - recv_ref[:, c * LANES : (c + 1) * LANES])
        high, low = split(residual, 2)
        placed = jnp.dot(low, weights, preferred_element_type=jnp.float32)
        placed = placed + jnp.dot(high, weights, preferred_element_type=jnp.float32)
        high, low = split(jnp.where(inside, pseudo_step * placed, 0.0), 2)
        high_ref[:, c * cols : (c + 1) * cols] = high
        low_ref[:, c * cols : (c + 1) * cols] = low


def place_lines(recv_ref, high_ref, low_ref, forcing_ref):
    slots = recv_ref.shape[0]
    lines = forcing_ref.shape[0]
    block = recv_ref[:, 3 * LANES :].T[1:2].astype(jnp.int32)
    step = 512
    for q in range(lines // step):
        number = lax.broadcasted_iota(jnp.int32, (step, slots), 0) + q * step
        chosen = (number == block).astype(jnp.bfloat16)
        for c in range(3):
            at = pl.ds(c * 256, 256)
            total = jnp.dot(chosen, low_ref[:, at], preferred_element_type=jnp.float32)
            total = total + jnp.dot(chosen, high_ref[:, at], preferred_element_type=jnp.float32)
            forcing_ref[q * step : (q + 1) * step, at] = total


def halves(x):
    return x[:, :LANES], x[:, LANES:]


def up_down(pair, below, above, first, last):
    left, right = pair
    left_up, right_up = pltpu.roll(left, LANES - 1, axis=1), pltpu.roll(right, LANES - 1, axis=1)
    left_down, right_down = pltpu.roll(left, 1, axis=1), pltpu.roll(right, 1, axis=1)
    up = (jnp.where(last, right_up, left_up), jnp.where(last, above, right_up))
    down = (jnp.where(first, below, left_down), jnp.where(first, left_down, right_down))
    return up, down


def sweep_plane(z, planes, rows, adj, ux, uy, uz, vv, yh, forcing, out, xe, ye):
    lanes = lane_iota()
    first, last = lanes == 0, lanes == LANES - 1
    here = z + 1

    def pair(ref, *index):
        return ref[(*index, slice(0, LANES))], ref[(*index, slice(LANES, 2 * LANES))]

    for r in range(rows // SUB):
        at = slice(r * SUB, (r + 1) * SUB)
        mid = slice(PAD + r * SUB, PAD + (r + 1) * SUB)
        plus = slice(PAD + r * SUB + 1, PAD + (r + 1) * SUB + 1)
        minus = slice(PAD + r * SUB - 1, PAD + (r + 1) * SUB - 1)
        edge_low, edge_high = yh[0, at, :], yh[1, at, :]

        def outside(k):
            lane = k * planes + z
            return (
                pltpu.roll(edge_low, LANES - lane, axis=1),
                pltpu.roll(edge_high, LANES - 1 - lane, axis=1),
            )

        v = pair(vv, here, mid)
        v_xp, v_xm = pair(vv, here, plus), pair(vv, here, minus)
        v_zp, v_zm = pair(vv, here + 1, mid), pair(vv, here - 1, mid)
        v_yp, v_ym = up_down(v, *outside(4), first, last)
        u_xp, u_xm = pair(ux, here, plus), pair(ux, here, minus)
        u_yp, u_ym = up_down(pair(uy, here, at), *outside(3), first, last)
        u_zp, u_zm = pair(uz, here + 1, at), pair(uz, here - 1, at)
        coef = []
        for h in range(2):
            n = [v[h] + w[h] for w in (v_xp, v_xm, v_yp, v_ym, v_zp, v_zm)]
            centre = 1.0 - ((n[0] + n[1]) + (n[2] + n[3]) + (n[4] + n[5]))
            coef.append(
                (
                    centre,
                    n[0] - u_xp[h],
                    n[1] + u_xm[h],
                    n[2] - u_yp[h],
                    n[3] + u_ym[h],
                    n[4] - u_zp[h],
                    n[5] + u_zm[h],
                )
            )
        if ye is not None:
            packed = [ye[0, at, :], ye[1, at, :]]
        for c in range(3):
            a = pair(adj, c, here, mid)
            a_xp, a_xm = pair(adj, c, here, plus), pair(adj, c, here, minus)
            a_zp, a_zm = pair(adj, c, here + 1, mid), pair(adj, c, here - 1, mid)
            a_yp, a_ym = up_down(a, *outside(c), first, last)
            new = []
            for h in range(2):
                k = coef[h]
                value = k[0] * a[h] + (k[1] * a_xp[h] + k[2] * a_xm[h])
                value = value + (k[3] * a_yp[h] + k[4] * a_ym[h])
                value = value + (k[5] * a_zp[h] + k[6] * a_zm[h])
                lane = c * 2 * LANES + h * LANES
                value = value + forcing(r, lane)
                out[c, z, at, h * LANES : (h + 1) * LANES] = value
                new.append(value)
            if ye is not None:
                lane = c * planes + z
                packed[0] = jnp.where(lanes == lane, pltpu.roll(new[0], lane, axis=1), packed[0])
                packed[1] = jnp.where(lanes == lane, pltpu.roll(new[1], lane + 1, axis=1), packed[1])
                for h in range(2):
                    half = slice(h * LANES, (h + 1) * LANES)
                    if r == 0:
                        put_row(xe, 0, lane, new[h][0:1], half)
                    if r == rows // SUB - 1:
                        put_row(xe, 1, lane, new[h][SUB - 1 : SUB], half)
        if ye is not None:
            ye[0, at, :], ye[1, at, :] = packed


def sweep_kernel(n_gx, n_gy, leading, *refs):
    if leading:
        (recv_in, weight_ref, vel_in, visc_in, adj_in, xh_ref, yh_ref,
         out_hbm, f_hbm, xe_ref, ye_ref,
         vel, visc, adj, ux, uy, uz, vv, yh, out, frc, high, low, load, save, fsave) = refs
    else:
        (f_hbm, vel_in, visc_in, adj_in, xh_ref, yh_ref, xa_ref, ya_ref,
         out_hbm,
         vel, visc, adj, ux, uy, uz, vv, yh, out, frc, load, save, fload) = refs
    planes, rows, cols = visc.shape
    gx, gy = lax.axis_index("gx"), lax.axis_index("gy")
    copies = []
    for z in range(planes):
        copies.append(
            [
                pltpu.make_async_copy(vel_in.at[:, z], vel.at[:, z], load.at[0, z]),
                pltpu.make_async_copy(visc_in.at[z], visc.at[z], load.at[1, z]),
                pltpu.make_async_copy(adj_in.at[:, z], adj.at[:, z + 1, pl.ds(PAD, rows), :], load.at[2, z]),
            ]
        )
    if leading:
        for which in range(3):
            for z in range(planes):
                copies[z][which].start()
    else:
        for z in range(planes):
            for copy in copies[z]:
                copy.start()
            pltpu.make_async_copy(
                f_hbm.at[pl.ds(z * rows, rows)], frc.at[pl.ds(z * rows, rows)], fload.at[z]
            ).start()
    zero = jnp.zeros((rows + 2 * PAD, cols), jnp.float32)
    for at in (0, planes + 1):
        vv[at] = zero
        uz[at] = zero[:rows]
        for c in range(3):
            adj[c, at] = zero
    inner = [
        (gx > 0).astype(jnp.float32),
        (gx < n_gx - 1).astype(jnp.float32),
        (gy > 0).astype(jnp.float32),
        (gy < n_gy - 1).astype(jnp.float32),
    ]
    lanes = lane_iota(rows)
    for side in range(2):
        packed = yh_ref[side] * inner[2 + side]
        packed = jnp.where(lanes < 3 * planes, packed, packed * half_step)
        if not leading:
            packed = jnp.where(lanes < 3 * planes, ya_ref[side] * inner[2 + side], packed)
        yh[side] = packed
    ends = ((0, PAD - 1), (1, PAD + rows))

    def fields(z):
        ux[z + 1, PAD : PAD + rows, :] = vel[0, z].astype(jnp.float32) * half_step
        uy[z + 1] = vel[1, z].astype(jnp.float32) * half_step
        uz[z + 1] = vel[2, z].astype(jnp.float32) * half_step
        vv[z + 1, PAD : PAD + rows, :] = visc[z].astype(jnp.float32) * half_step
        for side, at in ends:
            ux[z + 1, at : at + 1, :] = xh_ref[side, pl.ds(3 * planes + z, 1), :] * (inner[side] * half_step)
            vv[z + 1, at : at + 1, :] = xh_ref[side, pl.ds(4 * planes + z, 1), :] * (inner[side] * half_step)
            for c in range(3):
                edge = (xh_ref if leading else xa_ref)[side, pl.ds(c * planes + z, 1), :]
                adj[c, z + 1, at : at + 1, :] = edge * inner[side]

    def arrive(z):
        pltpu.make_async_copy(visc_in.at[z], visc.at[z], load.at[1, z]).wait()
        pltpu.make_async_copy(adj_in.at[:, z], adj.at[:, z + 1, pl.ds(PAD, rows), :], load.at[2, z]).wait()
        if not leading:
            pltpu.make_async_copy(vel_in.at[:, z], vel.at[:, z], load.at[0, z]).wait()

    if leading:
        xe_ref[...] = jnp.zeros_like(xe_ref)
        ye_ref[...] = jnp.zeros_like(ye_ref)
        for z in range(planes):
            copies[z][0].wait()
        line_forcing(recv_in, vel, weight_ref, high, low)
        place_lines(recv_in, high, low, frc)
        whole = pltpu.make_async_copy(frc, f_hbm, fsave)
        whole.start()
    arrive(0)
    fields(0)

    @pl.loop(0, planes)
    def _(z):
        @pl.when(z + 1 < planes)
        def _():
            arrive(z + 1)
            fields(z + 1)

        if not leading:
            pltpu.make_async_copy(
                f_hbm.at[pl.ds(z * rows, rows)], frc.at[pl.ds(z * rows, rows)], fload.at[z]
            ).wait()

        def forcing(r, lane):
            return frc[pl.ds(z * rows + r * SUB, SUB), pl.ds(lane, LANES)]

        sweep_plane(
            z, planes, rows, adj, ux, uy, uz, vv, yh, forcing, out,
            xe_ref if leading else None, ye_ref if leading else None,
        )
        pltpu.make_async_copy(out.at[:, z], out_hbm.at[:, z], save.at[z]).start()

    for z in range(planes):
        pltpu.make_async_copy(out.at[:, z], out_hbm.at[:, z], save.at[z]).wait()
    if leading:
        whole.wait()


def sweep(leading, n_gx, n_gy, *arrays):
    visc = arrays[3 if leading else 2]
    planes, rows, cols = visc.shape
    f32, bf16 = jnp.float32, jnp.bfloat16
    vmem = pl.BlockSpec(memory_space=pltpu.VMEM)
    any_space = pl.BlockSpec(memory_space=pl.ANY)
    result = jax.ShapeDtypeStruct((3, planes, rows, cols), f32)
    dma = pltpu.SemaphoreType.DMA
    scratch = [
        pltpu.VMEM((3, planes, rows, cols), bf16),
        pltpu.VMEM((planes, rows, cols), bf16),
        pltpu.VMEM((3, planes + 2, rows + 2 * PAD, cols), f32),
        pltpu.VMEM((planes + 2, rows + 2 * PAD, cols), f32),
        pltpu.VMEM((planes + 2, rows, cols), f32),
        pltpu.VMEM((planes + 2, rows, cols), f32),
        pltpu.VMEM((planes + 2, rows + 2 * PAD, cols), f32),
        pltpu.VMEM((2, rows, LANES), f32),
        pltpu.VMEM((3, planes, rows, cols), f32),
        pltpu.VMEM((planes * rows, 3 * cols), f32),
    ]
    if leading:
        slots = arrays[0].shape[0]
        scratch += [
            pltpu.VMEM((slots, 3 * cols), bf16),
            pltpu.VMEM((slots, 3 * cols), bf16),
            dma((3, planes)),
            dma((planes,)),
            dma,
        ]
        in_specs = [vmem, vmem, any_space, any_space, any_space, vmem, vmem]
        out_specs = [any_space, any_space, vmem, vmem]
        out_shape = [
            result,
            jax.ShapeDtypeStruct((planes * rows, 3 * cols), f32),
            jax.ShapeDtypeStruct((2, 3 * planes, cols), f32),
            jax.ShapeDtypeStruct((2, rows, LANES), f32),
        ]
    else:
        scratch += [dma((3, planes)), dma((planes,)), dma((planes,))]
        in_specs = [any_space] * 4 + [vmem] * 4
        out_specs, out_shape = any_space, result
    return pl.pallas_call(
        functools.partial(sweep_kernel, n_gx, n_gy, leading),
        name="sweep_first" if leading else "sweep_second",
        in_specs=in_specs,
        out_specs=out_specs,
        out_shape=out_shape,
        scratch_shapes=scratch,
        compiler_params=pltpu.CompilerParams(vmem_limit_bytes=60 << 20),
    )(*arrays)


def local(
    n_gx,
    n_gy,
    velocity,
    kinetic_energy,
    dissipation_rate,
    adjoint_start,
    interp_weight,
    observed,
    window_weight,
    window_source,
    window_block,
    window_count,
):
    peers = n_gx * n_gy
    windows = window_block.shape[0]
    meta = jnp.stack([window_source[:, 0], window_block, window_count]).astype(jnp.float32)
    meta = jnp.concatenate([meta, window_weight[None], jnp.zeros((4, windows), jnp.float32)])
    slots, visc, xe, ye = prep(
        meta, observed, velocity, kinetic_energy, dissipation_rate, adjoint_start, peers
    )
    received, xh, yh = exchange(
        xe, ye, slots.reshape(peers, CAP, 4 * LANES), n_gx, n_gy, 0
    )
    received = received.reshape(peers * CAP, 4 * LANES)
    adjoint, forcing, xe, ye = sweep(
        True, n_gx, n_gy, received, interp_weight, velocity, visc, adjoint_start, xh, yh
    )
    xa, ya = exchange(xe, ye, None, n_gx, n_gy, 1)
    return sweep(False, n_gx, n_gy, forcing, velocity, visc, adjoint, xh, yh, xa, ya)


def solution(mesh):
    placed = (
        P(None, None, "gx", "gy"),
        P(None, "gx", "gy"),
        P(None, "gx", "gy"),
        P(None, None, "gx", "gy"),
        P(),
        P(None, ("gx", "gy"), None),
        P(("gx", "gy")),
        P(("gx", "gy"), None),
        P(("gx", "gy")),
        P(("gx", "gy")),
    )
    return jax.shard_map(
        functools.partial(local, mesh.shape["gx"], mesh.shape["gy"]),
        mesh=mesh,
        in_specs=placed,
        out_specs=P(None, None, "gx", "gy"),
        check_vma=False,
    )
```

```python
import functools

import jax
import jax.numpy as jnp
from jax import lax
from jax.experimental import pallas as pl
from jax.experimental.pallas import tpu as pltpu
from jax.sharding import PartitionSpec as P

MESH = pl.DeviceIdType.MESH
SWEEPS = 2
CAP = 4
LANES = 128
SUB = 8

base_viscosity = 0.05
pseudo_step = 0.4
half_step = 0.5 * pseudo_step

HALF = 2 * LANES
BLOCK, COUNT, WEIGHT = 0, 1, 2
PAD = 8


def lane_iota(rows=SUB):
    return lax.broadcasted_iota(jnp.int32, (rows, LANES), 1)


def split(x, pieces):
    out = []
    for _ in range(pieces):
        piece = x.astype(jnp.bfloat16)
        out.append(piece)
        x = x - piece.astype(jnp.float32)
    return out


def fill_slots(source, block, count, weight, obs_ref, slots_ref):
    windows = source.shape[1]
    peers = slots_ref.shape[0]
    slots = peers * CAP
    f32 = jnp.float32
    meta = jnp.concatenate(
        [
            block.astype(f32),
            count.astype(f32),
            weight,
            source.astype(f32),
            jnp.zeros((LANES - 4, windows), f32),
        ],
        axis=0,
    ).T
    first = lax.broadcasted_iota(jnp.int32, (windows, windows), 0)
    second = lax.broadcasted_iota(jnp.int32, (windows, windows), 1)
    same = (meta[:, 3:4] == source.astype(f32)) & (first < second)
    place = jnp.sum(same.astype(f32), axis=0, keepdims=True).astype(jnp.int32)
    chosen = lax.broadcasted_iota(jnp.int32, (slots, windows), 0) == source * CAP + place
    chosen = chosen.astype(jnp.bfloat16)
    top = lax.broadcasted_iota(jnp.int32, (slots // SUB, SUB, LANES), 1) < CAP
    quarters = []
    for values in (obs_ref[0], obs_ref[1], obs_ref[2], meta):
        total = jnp.zeros((slots, LANES), f32)
        for piece in reversed(split(values, 3)):
            total = total + jnp.dot(chosen, piece, preferred_element_type=f32)
        quarters.append(total.reshape(slots // SUB, SUB, LANES))
    for h in range(2):
        upper, lower = quarters[h], quarters[2 + h]
        even = jnp.where(top, upper, pltpu.roll(lower, CAP, axis=1))
        odd = jnp.where(top, pltpu.roll(upper, CAP, axis=1), lower)
        slots_ref[:, :, h * LANES : (h + 1) * LANES] = jnp.stack([even, odd], axis=1).reshape(
            peers, SUB, LANES
        )


def read_slots(recv_ref):
    peers = recv_ref.shape[0]
    top = lax.broadcasted_iota(jnp.int32, (peers // 2, SUB, LANES), 1) < CAP
    quarters = [None] * 4
    for h in range(2):
        pairs = recv_ref[:, :, h * LANES : (h + 1) * LANES].reshape(peers // 2, 2, SUB, LANES)
        even, odd = pairs[:, 0], pairs[:, 1]
        upper = jnp.where(top, even, pltpu.roll(odd, CAP, axis=1))
        lower = jnp.where(top, pltpu.roll(even, CAP, axis=1), odd)
        quarters[h] = upper.reshape(peers * CAP, LANES)
        quarters[2 + h] = lower.reshape(peers * CAP, LANES)
    return quarters


def line_forcing(quarters, vel_ref, weight_ref, high_ref, low_ref):
    meta = quarters[3]
    slots = meta.shape[0]
    planes, rows, cols = vel_ref.shape[1:]
    weights = weight_ref[...]
    block = meta[:, BLOCK : BLOCK + 1].astype(jnp.int32)
    count = meta[:, COUNT : COUNT + 1].astype(jnp.int32)
    scale = meta[:, WEIGHT : WEIGHT + 1]
    inside = lax.broadcasted_iota(jnp.int32, (slots, cols), 1) < count
    group = 4
    lines = [jnp.zeros((slots, cols), jnp.float32) for _ in range(3)]
    for q in range(planes // group):
        number = lax.broadcasted_iota(jnp.int32, (slots, group * rows), 1) + q * group * rows
        chosen = (number == block).astype(jnp.bfloat16)
        for c in range(3):
            some = vel_ref[c, q * group : (q + 1) * group].reshape(group * rows, cols)
            lines[c] = lines[c] + jnp.dot(chosen, some, preferred_element_type=jnp.float32)
    for c in range(3):
        masked = jnp.where(inside, lines[c], 0.0).astype(jnp.bfloat16)
        predicted = lax.dot_general(
            masked, weights, (((1,), (1,)), ((), ())), preferred_element_type=jnp.float32
        )
        high, low = split(scale * (predicted - quarters[c]), 2)
        placed = jnp.dot(low, weights, preferred_element_type=jnp.float32)
        placed = placed + jnp.dot(high, weights, preferred_element_type=jnp.float32)
        high, low = split(jnp.where(inside, pseudo_step * placed, 0.0), 2)
        high_ref[:, c * cols : (c + 1) * cols] = high
        low_ref[:, c * cols : (c + 1) * cols] = low


GROUP = 4


def place_lines(q, block, high_ref, low_ref, forcing, out):
    slots = high_ref.shape[0]
    rows, cols = forcing.shape[2:]
    step = GROUP * rows
    number = lax.broadcasted_iota(jnp.int32, (step, slots), 0) + q * step
    chosen = (number == block).astype(jnp.bfloat16)
    at = slice(q * GROUP, (q + 1) * GROUP)
    for c in range(3):
        lanes = slice(c * cols, (c + 1) * cols)
        total = jnp.dot(chosen, low_ref[:, lanes], preferred_element_type=jnp.float32)
        total = total + jnp.dot(chosen, high_ref[:, lanes], preferred_element_type=jnp.float32)
        total = total.reshape(GROUP, rows, cols)
        forcing[c, at] = total
        out[c, at] = out[c, at] + total


def pack_edges(fields_x, fields_y, rows, cols, xe, ye):
    for k, read in enumerate(fields_x):
        xe[0, k : k + 1, :] = read(slice(0, 1), slice(0, cols))
        xe[1, k : k + 1, :] = read(slice(rows - 1, rows), slice(0, cols))
    lanes = lane_iota()

    @pl.loop(0, rows // SUB)
    def _(r):
        base = pl.multiple_of(r * SUB, SUB)
        low = jnp.zeros((SUB, LANES), jnp.float32)
        high = jnp.zeros((SUB, LANES), jnp.float32)
        for k, read in enumerate(fields_y):
            here = lanes == k
            first = pltpu.roll(read(pl.ds(base, SUB), slice(0, LANES)), k, axis=1)
            last = pltpu.roll(read(pl.ds(base, SUB), slice(cols - LANES, cols)), (k + 1) % LANES, axis=1)
            low = jnp.where(here, first, low)
            high = jnp.where(here, last, high)
        ye[0, pl.ds(base, SUB), :] = low
        ye[1, pl.ds(base, SUB), :] = high


def inside_flags(n_gx, n_gy):
    gx, gy = lax.axis_index("gx"), lax.axis_index("gy")
    flags = (gx > 0, gx < n_gx - 1, gy > 0, gy < n_gy - 1)
    return [flag.astype(jnp.float32) for flag in flags]


def shifted(rows, by):
    if isinstance(rows, slice):
        return slice(rows.start + by, rows.stop + by)
    return pl.ds(pl.multiple_of(rows.start + by, SUB), rows.size)


def clear_outside(planes, rows, cols, adj, uz, vv):
    zero = jnp.zeros((rows, cols), jnp.float32)
    for at in (0, planes + 1):
        vv[at, PAD : PAD + rows, :] = zero
        uz[at] = zero
        for c in range(3):
            adj[c, at, PAD : PAD + rows, :] = zero


def up_down(pair, below, above, first, last):
    left, right = pair
    left_up, right_up = pltpu.roll(left, LANES - 1, axis=1), pltpu.roll(right, LANES - 1, axis=1)
    left_down, right_down = pltpu.roll(left, 1, axis=1), pltpu.roll(right, 1, axis=1)
    up = (jnp.where(last, right_up, left_up), jnp.where(last, above, right_up))
    down = (jnp.where(first, below, left_down), jnp.where(first, left_down, right_down))
    return up, down


def sweep_plane(z, planes, rows, adj, ux, uy, uz, vv, yh, forcing, out):
    lanes = lane_iota()
    first, last = lanes == 0, lanes == LANES - 1
    here = z + 1

    def pair(ref, *index):
        return ref[(*index, slice(0, LANES))], ref[(*index, slice(LANES, 2 * LANES))]

    for r in range(rows // SUB):
        at = slice(r * SUB, (r + 1) * SUB)
        mid = slice(PAD + r * SUB, PAD + (r + 1) * SUB)
        plus = slice(PAD + r * SUB + 1, PAD + (r + 1) * SUB + 1)
        minus = slice(PAD + r * SUB - 1, PAD + (r + 1) * SUB - 1)
        edge_low, edge_high = yh[0, at, :], yh[1, at, :]

        def outside(k):
            lane = k * planes + z
            return (
                pltpu.roll(edge_low, LANES - lane, axis=1),
                pltpu.roll(edge_high, LANES - 1 - lane, axis=1),
            )

        v = pair(vv, here, mid)
        v_xp, v_xm = pair(vv, here, plus), pair(vv, here, minus)
        v_zp, v_zm = pair(vv, here + 1, mid), pair(vv, here - 1, mid)
        v_yp, v_ym = up_down(v, *outside(4), first, last)
        u_xp, u_xm = pair(ux, here, plus), pair(ux, here, minus)
        u_yp, u_ym = up_down(pair(uy, here, at), *outside(3), first, last)
        u_zp, u_zm = pair(uz, here + 1, at), pair(uz, here - 1, at)
        coef = []
        for h in range(2):
            n = [v[h] + w[h] for w in (v_xp, v_xm, v_yp, v_ym, v_zp, v_zm)]
            centre = 1.0 - ((n[0] + n[1]) + (n[2] + n[3]) + (n[4] + n[5]))
            coef.append(
                (
                    centre,
                    n[0] - u_xp[h],
                    n[1] + u_xm[h],
                    n[2] - u_yp[h],
                    n[3] + u_ym[h],
                    n[4] - u_zp[h],
                    n[5] + u_zm[h],
                )
            )
        for c in range(3):
            a = pair(adj, c, here, mid)
            a_xp, a_xm = pair(adj, c, here, plus), pair(adj, c, here, minus)
            a_zp, a_zm = pair(adj, c, here + 1, mid), pair(adj, c, here - 1, mid)
            a_yp, a_ym = up_down(a, *outside(c), first, last)
            for h in range(2):
                k = coef[h]
                value = k[0] * a[h] + (k[1] * a_xp[h] + k[2] * a_xm[h])
                value = value + (k[3] * a_yp[h] + k[4] * a_ym[h])
                value = value + (k[5] * a_zp[h] + k[6] * a_zm[h])
                half = slice(h * LANES, (h + 1) * LANES)
                if forcing is not None:
                    value = value + forcing[c, z, at, half]
                out[c, z, at, half] = value


def first_kernel(n_gx, n_gy, *refs):
    (source, block, count, weight, obs, weights, vel_in, ke_in, dr_in, adj_in,
     out_hbm, f_hbm, visc_hbm, xh, yh, xa, ya,
     slots, recv, vel, ke, dr, visc, adj, ux, uy, uz, vv, yhs, out, frc, high, low, xe, ye, xe2, ye2,
     load, save, all_send, all_recv, local_sem, send, received) = refs
    planes, rows, cols = visc.shape
    peers = n_gx * n_gy
    gx, gy = lax.axis_index("gx"), lax.axis_index("gy")
    me = gx * n_gy + gy

    def device(step):
        peer = lax.rem(me + step, peers)
        return peer, (peer // n_gy, lax.rem(peer, n_gy))

    lower_x = (lax.rem(gx + n_gx - 1, n_gx), gy)
    upper_x = (lax.rem(gx + 1, n_gx), gy)
    lower_y = (gx, lax.rem(gy + n_gy - 1, n_gy))
    upper_y = (gx, lax.rem(gy + 1, n_gy))

    def edge_copies(turn, x_from, y_from, x_to, y_to):
        sides = (
            (x_from.at[1], x_to.at[0], upper_x),
            (x_from.at[0], x_to.at[1], lower_x),
            (y_from.at[1], y_to.at[0], upper_y),
            (y_from.at[0], y_to.at[1], lower_y),
        )
        return [
            pltpu.make_async_remote_copy(
                here, there, send.at[turn, k], received.at[turn, k], device_id=where, device_id_type=MESH
            )
            for k, (here, there, where) in enumerate(sides)
        ]

    adj_inner = adj.at[:, pl.ds(1, planes), pl.ds(PAD, rows), :]
    loads = [
        pltpu.make_async_copy(ke_in, ke, load.at[0]),
        pltpu.make_async_copy(dr_in, dr, load.at[1]),
        pltpu.make_async_copy(vel_in, vel, load.at[2]),
        pltpu.make_async_copy(adj_in, adj_inner, load.at[3]),
    ]
    for copy in loads:
        copy.start()
    barrier = pltpu.get_barrier_semaphore()

    @pl.loop(1, peers)
    def _(step):
        pl.semaphore_signal(barrier, inc=1, device_id=device(step)[1], device_id_type=MESH)

    fill_slots(source[...], block[...], count[...], weight[...], obs, slots)
    pl.semaphore_wait(barrier, peers - 1)
    own = pltpu.make_async_copy(slots.at[me], recv.at[me], local_sem)
    own.start()

    @pl.loop(1, peers)
    def _(step):
        peer, where = device(step)
        pltpu.make_async_remote_copy(
            slots.at[peer], recv.at[me], all_send, all_recv, device_id=where, device_id_type=MESH
        ).start()

    clear_outside(planes, rows, cols, adj, uz, vv)
    for copy in loads[:3]:
        copy.wait()

    @pl.loop(0, planes)
    def _(z):
        value = base_viscosity + ke[z].astype(jnp.float32) / dr[z].astype(jnp.float32)
        value = value.astype(jnp.bfloat16)
        visc[z] = value
        vv[z + 1, PAD : PAD + rows, :] = value.astype(jnp.float32) * half_step
        ux[z + 1, PAD : PAD + rows, :] = vel[0, z].astype(jnp.float32) * half_step
        uy[z + 1] = vel[1, z].astype(jnp.float32) * half_step
        uz[z + 1] = vel[2, z].astype(jnp.float32) * half_step

    visc_save = pltpu.make_async_copy(visc, visc_hbm, save.at[8])
    visc_save.start()
    loads[3].wait()

    def of_adj(c, z):
        return lambda at, lanes: adj[c, z + 1, shifted(at, PAD), lanes]

    def padded(ref, z):
        return lambda at, lanes: ref[z + 1, shifted(at, PAD), lanes]

    def of_uy(z):
        return lambda at, lanes: uy[z + 1, at, lanes]

    starts = [of_adj(c, z) for c in range(3) for z in range(planes)]
    visc_fields = [padded(vv, z) for z in range(planes)]
    pack_edges(
        starts + [padded(ux, z) for z in range(planes)] + visc_fields,
        starts + [of_uy(z) for z in range(planes)] + visc_fields,
        rows, cols, xe, ye,
    )
    copies = edge_copies(0, xe, ye, xh, yh)
    for copy in copies:
        copy.start()
    for copy in copies:
        copy.wait()
    inner = inside_flags(n_gx, n_gy)
    for side, at in ((0, PAD - 1), (1, PAD + rows)):
        for z in range(planes):
            for c in range(3):
                k = c * planes + z
                adj[c, z + 1, at : at + 1, :] = xh[side, k : k + 1, :] * inner[side]
            k = 3 * planes + z
            ux[z + 1, at : at + 1, :] = xh[side, k : k + 1, :] * inner[side]
            k = 4 * planes + z
            vv[z + 1, at : at + 1, :] = xh[side, k : k + 1, :] * inner[side]
        yhs[side] = yh[side] * inner[2 + side]

    @pl.loop(0, planes)
    def _(z):
        sweep_plane(z, planes, rows, adj, ux, uy, uz, vv, yhs, None, out)

    own.wait()
    rest = pl.ds(0, peers - 1)
    pltpu.make_async_copy(slots.at[rest], slots.at[rest], all_send).wait()
    pltpu.make_async_copy(recv.at[rest], recv.at[rest], all_recv).wait()
    quarters = read_slots(recv)
    line_forcing(quarters, vel, weights, high, low)
    line_row = quarters[3].T[BLOCK : BLOCK + 1].astype(jnp.int32)
    saves = []
    for q in range(planes // GROUP):
        place_lines(q, line_row, high, low, frc, out)
        at = pl.ds(q * GROUP, GROUP)
        saves.append(pltpu.make_async_copy(frc.at[:, at], f_hbm.at[:, at], save.at[2 * q]))
        saves.append(pltpu.make_async_copy(out.at[:, at], out_hbm.at[:, at], save.at[2 * q + 1]))
        for copy in saves[-2:]:
            copy.start()

    def of_out(c, z):
        return lambda at, lanes: out[c, z, at, lanes]

    news = [of_out(c, z) for c in range(3) for z in range(planes)]
    pack_edges(news, news, rows, cols, xe2, ye2)
    copies = edge_copies(1, xe2, ye2, xa, ya)
    for copy in copies:
        copy.start()
    for copy in copies:
        copy.wait()
    for copy in saves:
        copy.wait()
    visc_save.wait()


def second_kernel(n_gx, n_gy, starts, *refs):
    (f_in, vel_in, visc_in, adj_in, xh, yh, xa, ya,
     out_hbm,
     vel, visc, adj, ux, uy, uz, vv, yhs, out, frc, load, save) = refs
    planes, rows, cols = visc.shape
    ends = starts[1:] + (planes,)

    def group(g):
        here = pl.ds(starts[g], ends[g] - starts[g])
        there = pl.ds(starts[g] + 1, ends[g] - starts[g])
        return [
            pltpu.make_async_copy(vel_in.at[:, here], vel.at[:, here], load.at[0, g]),
            pltpu.make_async_copy(visc_in.at[here], visc.at[here], load.at[1, g]),
            pltpu.make_async_copy(adj_in.at[:, here], adj.at[:, there, pl.ds(PAD, rows), :], load.at[2, g]),
            pltpu.make_async_copy(f_in.at[:, here], frc.at[:, here], load.at[3, g]),
        ]

    groups = [group(g) for g in range(len(starts))]
    for copies in groups:
        for copy in copies:
            copy.start()
    clear_outside(planes, rows, cols, adj, uz, vv)
    inner = inside_flags(n_gx, n_gy)
    lanes = lane_iota(rows)
    for side, at in ((0, PAD - 1), (1, PAD + rows)):
        for z in range(planes):
            for c in range(3):
                k = c * planes + z
                adj[c, z + 1, at : at + 1, :] = xa[side, k : k + 1, :] * inner[side]
            k = 3 * planes + z
            ux[z + 1, at : at + 1, :] = xh[side, k : k + 1, :] * inner[side]
            k = 4 * planes + z
            vv[z + 1, at : at + 1, :] = xh[side, k : k + 1, :] * inner[side]
        yhs[side] = jnp.where(lanes < 3 * planes, ya[side], yh[side]) * inner[2 + side]

    def fields(z):
        ux[z + 1, PAD : PAD + rows, :] = vel[0, z].astype(jnp.float32) * half_step
        uy[z + 1] = vel[1, z].astype(jnp.float32) * half_step
        uz[z + 1] = vel[2, z].astype(jnp.float32) * half_step
        vv[z + 1, PAD : PAD + rows, :] = visc[z].astype(jnp.float32) * half_step

    for copy in groups[0]:
        copy.wait()
    fields(0)

    @pl.loop(0, planes)
    def _(z):
        for g in range(1, len(starts)):

            @pl.when(z + 1 == starts[g])
            def _():
                for copy in groups[g]:
                    copy.wait()

        @pl.when(z + 1 < planes)
        def _():
            fields(z + 1)

        sweep_plane(z, planes, rows, adj, ux, uy, uz, vv, yhs, frc, out)
        pltpu.make_async_copy(out.at[:, z], out_hbm.at[:, z], save).start()

    pltpu.make_async_copy(out, out_hbm, save).wait()


def field_scratch(planes, rows, cols):
    f32, bf16 = jnp.float32, jnp.bfloat16
    tall = rows + 2 * PAD
    return [
        pltpu.VMEM((planes, rows, cols), bf16),
        pltpu.VMEM((3, planes + 2, tall, cols), f32),
        pltpu.VMEM((planes + 2, tall, cols), f32),
        pltpu.VMEM((planes + 2, rows, cols), f32),
        pltpu.VMEM((planes + 2, rows, cols), f32),
        pltpu.VMEM((planes + 2, tall, cols), f32),
        pltpu.VMEM((2, rows, LANES), f32),
        pltpu.VMEM((3, planes, rows, cols), f32),
        pltpu.VMEM((3, planes, rows, cols), f32),
    ]


def local(
    n_gx,
    n_gy,
    velocity,
    kinetic_energy,
    dissipation_rate,
    adjoint_start,
    interp_weight,
    observed,
    window_weight,
    window_source,
    window_block,
    window_count,
):
    planes, rows, cols = kinetic_energy.shape
    peers = n_gx * n_gy
    windows = window_block.shape[0]
    f32, bf16 = jnp.float32, jnp.bfloat16
    shape = jax.ShapeDtypeStruct
    vmem = pl.BlockSpec(memory_space=pltpu.VMEM)
    hbm = pl.BlockSpec(memory_space=pl.ANY)
    dma = pltpu.SemaphoreType.DMA
    whole = shape(adjoint_start.shape, f32)
    edges = [
        shape((2, 5 * planes, cols), f32),
        shape((2, rows, LANES), f32),
        shape((2, 3 * planes, cols), f32),
        shape((2, rows, LANES), f32),
    ]
    flat = (1, windows)
    adjoint, forcing, visc, xh, yh, xa, ya = pl.pallas_call(
        functools.partial(first_kernel, n_gx, n_gy),
        name="route_and_first_sweep",
        in_specs=[vmem] * 6 + [hbm] * 4,
        out_specs=[hbm] * 3 + [vmem] * 4,
        out_shape=[whole, whole, shape((planes, rows, cols), bf16)] + edges,
        scratch_shapes=[
            pltpu.VMEM((peers, SUB, HALF), f32),
            pltpu.VMEM((peers, SUB, HALF), f32),
            pltpu.VMEM((3, planes, rows, cols), bf16),
            pltpu.VMEM((planes, rows, cols), bf16),
            pltpu.VMEM((planes, rows, cols), bf16),
        ]
        + field_scratch(planes, rows, cols)
        + [
            pltpu.VMEM((peers * CAP, 3 * cols), bf16),
            pltpu.VMEM((peers * CAP, 3 * cols), bf16),
        ]
        + [pltpu.VMEM(e.shape, e.dtype) for e in edges]
        + [dma((4,)), dma((2 * planes // GROUP + 1,)), dma, dma, dma, dma((2, 4)), dma((2, 4))],
        compiler_params=pltpu.CompilerParams(
            collective_id=0, has_side_effects=True, vmem_limit_bytes=60 << 20
        ),
    )(
        window_source.reshape(flat),
        window_block.reshape(flat),
        window_count.reshape(flat),
        window_weight.reshape(flat),
        observed,
        interp_weight,
        velocity,
        kinetic_energy,
        dissipation_rate,
        adjoint_start,
    )
    starts = (0, 1, 2, 4, 8, 12)
    return pl.pallas_call(
        functools.partial(second_kernel, n_gx, n_gy, starts),
        name="second_sweep",
        in_specs=[hbm] * 4 + [vmem] * 4,
        out_specs=hbm,
        out_shape=whole,
        scratch_shapes=[pltpu.VMEM((3, planes, rows, cols), bf16)]
        + field_scratch(planes, rows, cols)
        + [dma((4, len(starts))), dma],
        compiler_params=pltpu.CompilerParams(vmem_limit_bytes=60 << 20),
    )(forcing, velocity, visc, adjoint, xh, yh, xa, ya)


def solution(mesh):
    placed = (
        P(None, None, "gx", "gy"),
        P(None, "gx", "gy"),
        P(None, "gx", "gy"),
        P(None, None, "gx", "gy"),
        P(),
        P(None, ("gx", "gy"), None),
        P(("gx", "gy")),
        P(("gx", "gy"), None),
        P(("gx", "gy")),
        P(("gx", "gy")),
    )
    return jax.shard_map(
        functools.partial(local, mesh.shape["gx"], mesh.shape["gy"]),
        mesh=mesh,
        in_specs=placed,
        out_specs=P(None, None, "gx", "gy"),
        check_vma=False,
    )
```

```python
import functools

import jax
import jax.numpy as jnp
from jax import lax
from jax.experimental import pallas as pl
from jax.experimental.pallas import tpu as pltpu
from jax.sharding import PartitionSpec as P

MESH = pl.DeviceIdType.MESH
SWEEPS = 2
CAP = 4
LANES = 128
SUB = 8

base_viscosity = 0.05
pseudo_step = 0.4
half_step = 0.5 * pseudo_step

HALF = 2 * LANES
BLOCK, COUNT, WEIGHT = 0, 1, 2
PAD = 8


def lane_iota(rows=SUB):
    return lax.broadcasted_iota(jnp.int32, (rows, LANES), 1)


def split(x, pieces):
    out = []
    for _ in range(pieces):
        piece = x.astype(jnp.bfloat16)
        out.append(piece)
        x = x - piece.astype(jnp.float32)
    return out


def fill_slots(source, block, count, weight, obs_ref, slots_ref):
    windows = source.shape[1]
    peers = slots_ref.shape[0]
    slots = peers * CAP
    f32 = jnp.float32
    meta = jnp.concatenate(
        [
            block.astype(f32),
            count.astype(f32),
            weight,
            source.astype(f32),
            jnp.zeros((LANES - 4, windows), f32),
        ],
        axis=0,
    ).T
    first = lax.broadcasted_iota(jnp.int32, (windows, windows), 0)
    second = lax.broadcasted_iota(jnp.int32, (windows, windows), 1)
    same = (meta[:, 3:4] == source.astype(f32)) & (first < second)
    place = jnp.sum(same.astype(f32), axis=0, keepdims=True).astype(jnp.int32)
    chosen = lax.broadcasted_iota(jnp.int32, (slots, windows), 0) == source * CAP + place
    chosen = chosen.astype(jnp.bfloat16)
    top = lax.broadcasted_iota(jnp.int32, (slots // SUB, SUB, LANES), 1) < CAP
    quarters = []
    for values in (obs_ref[0], obs_ref[1], obs_ref[2], meta):
        total = jnp.zeros((slots, LANES), f32)
        for piece in reversed(split(values, 3)):
            total = total + jnp.dot(chosen, piece, preferred_element_type=f32)
        quarters.append(total.reshape(slots // SUB, SUB, LANES))
    for h in range(2):
        upper, lower = quarters[h], quarters[2 + h]
        even = jnp.where(top, upper, pltpu.roll(lower, CAP, axis=1))
        odd = jnp.where(top, pltpu.roll(upper, CAP, axis=1), lower)
        slots_ref[:, :, h * LANES : (h + 1) * LANES] = jnp.stack([even, odd], axis=1).reshape(
            peers, SUB, LANES
        )


def read_slots(recv_ref):
    peers = recv_ref.shape[0]
    top = lax.broadcasted_iota(jnp.int32, (peers // 2, SUB, LANES), 1) < CAP
    quarters = [None] * 4
    for h in range(2):
        pairs = recv_ref[:, :, h * LANES : (h + 1) * LANES].reshape(peers // 2, 2, SUB, LANES)
        even, odd = pairs[:, 0], pairs[:, 1]
        upper = jnp.where(top, even, pltpu.roll(odd, CAP, axis=1))
        lower = jnp.where(top, pltpu.roll(even, CAP, axis=1), odd)
        quarters[h] = upper.reshape(peers * CAP, LANES)
        quarters[2 + h] = lower.reshape(peers * CAP, LANES)
    return quarters


def line_forcing(quarters, vel_ref, weight_ref, high_ref, low_ref):
    meta = quarters[3]
    slots = meta.shape[0]
    planes, rows, cols = vel_ref.shape[1:]
    weights = weight_ref[...]
    block = meta[:, BLOCK : BLOCK + 1].astype(jnp.int32)
    count = meta[:, COUNT : COUNT + 1].astype(jnp.int32)
    scale = meta[:, WEIGHT : WEIGHT + 1]
    inside = lax.broadcasted_iota(jnp.int32, (slots, cols), 1) < count
    group = 4
    lines = [jnp.zeros((slots, cols), jnp.float32) for _ in range(3)]
    for q in range(planes // group):
        number = lax.broadcasted_iota(jnp.int32, (slots, group * rows), 1) + q * group * rows
        chosen = (number == block).astype(jnp.bfloat16)
        for c in range(3):
            some = vel_ref[c, q * group : (q + 1) * group].reshape(group * rows, cols)
            lines[c] = lines[c] + jnp.dot(chosen, some, preferred_element_type=jnp.float32)
    edge_values = []
    for c in range(3):
        masked = jnp.where(inside, lines[c], 0.0).astype(jnp.bfloat16)
        predicted = lax.dot_general(
            masked, weights, (((1,), (1,)), ((), ())), preferred_element_type=jnp.float32
        )
        high, low = split(scale * (predicted - quarters[c]), 2)
        placed = jnp.dot(low, weights, preferred_element_type=jnp.float32)
        placed = placed + jnp.dot(high, weights, preferred_element_type=jnp.float32)
        placed = jnp.where(inside, pseudo_step * placed, 0.0)
        edge_values.append((placed[:, 0:1], placed[:, cols - 1 : cols]))
        high, low = split(placed, 2)
        high_ref[:, c * cols : (c + 1) * cols] = high
        low_ref[:, c * cols : (c + 1) * cols] = low
    return edge_values


def force_edges(block, meta, edge_values, high_ref, low_ref, planes, rows, xe, ye):
    f32, bf16 = jnp.float32, jnp.bfloat16
    slots, width = high_ref.shape
    cols = width // 3
    number = lax.broadcasted_iota(jnp.int32, (2 * planes, slots), 0)
    line = number % planes * rows + number // planes * (rows - 1)
    chosen = (line == block).astype(bf16)
    total = jnp.dot(chosen, low_ref[...], preferred_element_type=f32)
    total = total + jnp.dot(chosen, high_ref[...], preferred_element_type=f32)
    for side in range(2):
        for c in range(3):
            at = slice(c * planes, (c + 1) * planes)
            xe[side, at, :] = xe[side, at, :] + total[side * planes : (side + 1) * planes, c * cols : (c + 1) * cols]
    lanes = lane_iota(slots)
    plane = meta[:, BLOCK : BLOCK + 1].astype(jnp.int32) // rows
    values = jnp.zeros((slots, LANES), f32)
    for c in range(3):
        for side in range(2):
            values = jnp.where(lanes // (2 * planes) * 2 + (1 - lanes % 2) == 2 * c + side, edge_values[c][side], values)
    values = jnp.where((lanes // 2 % planes == plane) & (lanes < 6 * planes), values, 0.0)
    chosen = (lax.broadcasted_iota(jnp.int32, (rows, slots), 0) == block % rows).astype(bf16)
    total = ye[...]
    for piece in reversed(split(values, 2)):
        total = total + jnp.dot(chosen, piece, preferred_element_type=f32)
    ye[...] = total


GROUP = 4


def place_lines(q, block, high_ref, low_ref, forcing, out):
    slots = high_ref.shape[0]
    rows, cols = forcing.shape[2:]
    step = GROUP * rows
    number = lax.broadcasted_iota(jnp.int32, (step, slots), 0) + q * step
    chosen = (number == block).astype(jnp.bfloat16)
    at = slice(q * GROUP, (q + 1) * GROUP)
    for c in range(3):
        lanes = slice(c * cols, (c + 1) * cols)
        total = jnp.dot(chosen, low_ref[:, lanes], preferred_element_type=jnp.float32)
        total = total + jnp.dot(chosen, high_ref[:, lanes], preferred_element_type=jnp.float32)
        total = total.reshape(GROUP, rows, cols)
        forcing[c, at] = total
        out[c, at] = out[c, at] + total


def pack_rows(fields, rows, cols, xe):
    for k, read in enumerate(fields):
        for h in range(2):
            half = slice(h * LANES, (h + 1) * LANES)
            xe[0, k : k + 1, half] = read(slice(0, 1), h)
            xe[1, k : k + 1, half] = read(slice(rows - 1, rows), h)


def pack_columns(fields, rows, ye):
    lanes = lane_iota()

    @pl.loop(0, rows // SUB)
    def _(r):
        at = pl.ds(pl.multiple_of(r * SUB, SUB), SUB)
        packed = jnp.zeros((SUB, LANES), jnp.float32)
        for k, read in fields:
            ends = jnp.where(lanes == 0, read(at, 0), read(at, 1))
            ends = pltpu.roll(ends, (2 * k + 1) % LANES, axis=1)
            packed = jnp.where(lanes // 2 == k, ends, packed)
        ye[at, :] = packed


def from_sides(yh, index):
    inner = inside_flags(*index)
    below = pltpu.roll(yh[0], 1, axis=1) * inner[2]
    above = pltpu.roll(yh[1], LANES - 1, axis=1) * inner[3]
    return jnp.where(lane_iota(below.shape[0]) % 2 == 1, below, above)


def inside_flags(n_gx, n_gy):
    gx, gy = lax.axis_index("gx"), lax.axis_index("gy")
    flags = (gx > 0, gx < n_gx - 1, gy > 0, gy < n_gy - 1)
    return [flag.astype(jnp.float32) for flag in flags]


def shifted(rows, by):
    if isinstance(rows, slice):
        return slice(rows.start + by, rows.stop + by)
    return pl.ds(pl.multiple_of(rows.start + by, SUB), rows.size)


def clear_outside(planes, rows, cols, adj, uz, vv):
    zero = jnp.zeros((rows, cols), jnp.float32)
    for at in (0, planes + 1):
        uz[at] = zero
        for h in range(2):
            vv[at, h, PAD : PAD + rows, :] = zero[:, :LANES]
            for c in range(3):
                adj[c, at, h, PAD : PAD + rows, :] = zero[:, :LANES]


def set_fields(z, vel, visc, ux, uy, uz, vv):
    rows = visc.shape[1]
    uy[z + 1] = vel[1, z].astype(jnp.float32) * half_step
    uz[z + 1] = vel[2, z].astype(jnp.float32) * half_step
    for h in range(2):
        half = slice(h * LANES, (h + 1) * LANES)
        vv[z + 1, h, PAD : PAD + rows, :] = visc[z, :, half].astype(jnp.float32) * half_step
        ux[z + 1, h, PAD : PAD + rows, :] = vel[0, z, :, half].astype(jnp.float32) * half_step


def set_rows(planes, rows, index, xa, xh, adj, ux, vv):
    inner = inside_flags(*index)
    for side, at in ((0, PAD - 1), (1, PAD + rows)):
        for z in range(planes):
            for h in range(2):
                half = slice(h * LANES, (h + 1) * LANES)
                for c in range(3):
                    k = c * planes + z
                    adj[c, z + 1, h, at : at + 1, :] = xa[side, k : k + 1, half] * inner[side]
                k = 3 * planes + z
                ux[z + 1, h, at : at + 1, :] = xh[side, k : k + 1, half] * inner[side]
                k = 4 * planes + z
                vv[z + 1, h, at : at + 1, :] = xh[side, k : k + 1, half] * inner[side]


def up_down(pair, outer, first, last):
    left, right = pair
    left_up, right_up = (pltpu.roll(x, LANES - 1, axis=1) for x in pair)
    left_down, right_down = (pltpu.roll(x, 1, axis=1) for x in pair)
    up = (jnp.where(last, right_up, left_up), jnp.where(last, outer, right_up))
    down = (jnp.where(first, outer, left_down), jnp.where(first, left_down, right_down))
    return up, down


def sweep_plane(z, planes, rows, adj, ux, uy, uz, vv, yhs, forcing, out):
    lanes = lane_iota()
    first, last = lanes == 0, lanes == LANES - 1
    here = z + 1
    both = (slice(0, LANES), slice(LANES, 2 * LANES))

    for r in range(rows // SUB):
        at = slice(r * SUB, (r + 1) * SUB)
        mid, plus, minus = (slice(at.start + PAD + d, at.stop + PAD + d) for d in (0, 1, -1))
        edges = [yhs[0, at, :], yhs[1, at, :]]

        def outer(which, k):
            return pltpu.roll(edges[which], LANES - 1 - 2 * (k * planes + z), axis=1)

        v = [vv[here, h, mid, :] for h in range(2)]
        v_yp, v_ym = up_down(v, outer(0, 3), first, last)
        u_yp, u_ym = up_down([uy[here, at, half] for half in both], outer(1, 3), first, last)
        coef = []
        for h in range(2):
            n_xp, n_xm = v[h] + vv[here, h, plus, :], v[h] + vv[here, h, minus, :]
            n_yp, n_ym = v[h] + v_yp[h], v[h] + v_ym[h]
            n_zp, n_zm = v[h] + vv[here + 1, h, mid, :], v[h] + vv[here - 1, h, mid, :]
            coef.append(
                (
                    1.0 - ((n_xp + n_xm) + (n_yp + n_ym) + (n_zp + n_zm)),
                    n_xp - ux[here, h, plus, :],
                    n_xm + ux[here, h, minus, :],
                    n_yp - u_yp[h],
                    n_ym + u_ym[h],
                    n_zp - uz[here + 1, at, both[h]],
                    n_zm + uz[here - 1, at, both[h]],
                )
            )
        for c in range(3):
            a = [adj[c, here, h, mid, :] for h in range(2)]
            a_yp, a_ym = up_down(a, outer(0, c), first, last)
            for h in range(2):
                k = coef[h]
                value = k[0] * a[h] + (k[1] * adj[c, here, h, plus, :] + k[2] * adj[c, here, h, minus, :])
                value = value + (k[3] * a_yp[h] + k[4] * a_ym[h])
                value = value + (k[5] * adj[c, here + 1, h, mid, :] + k[6] * adj[c, here - 1, h, mid, :])
                if forcing is not None:
                    value = value + forcing[c, z, at, both[h]]
                out[c, z, at, both[h]] = value


def first_kernel(n_gx, n_gy, *refs):
    (source, block, count, weight, obs, weights, vel_in, ke_in, dr_in, adj_in,
     out_hbm, f_hbm, visc_hbm, xh, yc, xa, ya,
     slots, recv, vel, ke, dr, visc, adj, ux, uy, uz, vv, yhs, out, frc, high, low, xe, ye, yh, xe2, ye2,
     load, save, all_send, all_recv, local_sem, send, received) = refs
    planes, rows, cols = visc.shape
    peers = n_gx * n_gy
    gx, gy = lax.axis_index("gx"), lax.axis_index("gy")
    me = gx * n_gy + gy

    def device(step):
        peer = lax.rem(me + step, peers)
        return peer, (peer // n_gy, lax.rem(peer, n_gy))

    lower_x = (lax.rem(gx + n_gx - 1, n_gx), gy)
    upper_x = (lax.rem(gx + 1, n_gx), gy)
    lower_y = (gx, lax.rem(gy + n_gy - 1, n_gy))
    upper_y = (gx, lax.rem(gy + 1, n_gy))

    def edge_copies(turn, x_from, y_from, x_to, y_to):
        sides = (
            (x_from.at[1], x_to.at[0], upper_x),
            (x_from.at[0], x_to.at[1], lower_x),
            (y_from, y_to.at[0], upper_y),
            (y_from, y_to.at[1], lower_y),
        )
        return [
            pltpu.make_async_remote_copy(
                here, there, send.at[turn, k], received.at[turn, k], device_id=where, device_id_type=MESH
            )
            for k, (here, there, where) in enumerate(sides)
        ]

    loads = [
        pltpu.make_async_copy(ke_in, ke, load.at[0]),
        pltpu.make_async_copy(dr_in, dr, load.at[1]),
        pltpu.make_async_copy(vel_in, vel, load.at[2]),
    ] + [
        pltpu.make_async_copy(
            adj_in.at[:, :, :, pl.ds(h * LANES, LANES)],
            adj.at[:, pl.ds(1, planes), h, pl.ds(PAD, rows), :],
            load.at[3 + h],
        )
        for h in range(2)
    ]
    for copy in loads:
        copy.start()
    barrier = pltpu.get_barrier_semaphore()

    @pl.loop(1, peers)
    def _(step):
        pl.semaphore_signal(barrier, inc=1, device_id=device(step)[1], device_id_type=MESH)

    fill_slots(source[...], block[...], count[...], weight[...], obs, slots)
    clear_outside(planes, rows, cols, adj, uz, vv)
    for copy in loads[:3]:
        copy.wait()

    @pl.loop(0, planes)
    def _(z):
        value = base_viscosity + ke[z].astype(jnp.float32) / dr[z].astype(jnp.float32)
        visc[z] = value.astype(jnp.bfloat16)
        set_fields(z, vel, visc, ux, uy, uz, vv)

    visc_save = pltpu.make_async_copy(visc, visc_hbm, save.at[8])
    visc_save.start()
    for copy in loads[3:]:
        copy.wait()

    def of_adj(c, z):
        return lambda at, h: adj[c, z + 1, h, shifted(at, PAD), :]

    def of_tall(ref, z):
        return lambda at, h: ref[z + 1, h, shifted(at, PAD), :]

    def of_uy(z):
        return lambda at, h: uy[z + 1, at, slice(h * LANES, (h + 1) * LANES)]

    starts = [of_adj(c, z) for c in range(3) for z in range(planes)]
    visc_fields = [of_tall(vv, z) for z in range(planes)]
    pack_rows(starts + [of_tall(ux, z) for z in range(planes)] + visc_fields, rows, cols, xe)
    pack_columns(list(enumerate(starts + visc_fields)), rows, ye.at[0])
    pack_columns([(3 * planes + z, of_uy(z)) for z in range(planes)], rows, ye.at[1])

    pl.semaphore_wait(barrier, peers - 1)
    copies = edge_copies(0, xe, ye, xh, yh)
    for copy in copies:
        copy.start()
    own = pltpu.make_async_copy(slots.at[me], recv.at[me], local_sem)
    own.start()

    @pl.loop(1, peers)
    def _(step):
        peer, where = device(step)
        pltpu.make_async_remote_copy(
            slots.at[peer], recv.at[me], all_send, all_recv, device_id=where, device_id_type=MESH
        ).start()

    for copy in copies:
        copy.wait()
    index = (n_gx, n_gy)
    set_rows(planes, rows, index, xh, xh, adj, ux, vv)
    for k in range(2):
        sides = from_sides(yh.at[:, k], index)
        yc[k] = sides
        yhs[k] = sides

    @pl.loop(0, planes)
    def _(z):
        sweep_plane(z, planes, rows, adj, ux, uy, uz, vv, yhs, None, out)

    def of_out(c, z):
        return lambda at, h: out[c, z, at, slice(h * LANES, (h + 1) * LANES)]

    news = [of_out(c, z) for c in range(3) for z in range(planes)]
    pack_rows(news, rows, cols, xe2)
    pack_columns(list(enumerate(news)), rows, ye2)

    own.wait()
    rest = pl.ds(0, peers - 1)
    pltpu.make_async_copy(slots.at[rest], slots.at[rest], all_send).wait()
    pltpu.make_async_copy(recv.at[rest], recv.at[rest], all_recv).wait()
    quarters = read_slots(recv)
    edge_values = line_forcing(quarters, vel, weights, high, low)
    block = quarters[3].T[BLOCK : BLOCK + 1].astype(jnp.int32)
    force_edges(block, quarters[3], edge_values, high, low, planes, rows, xe2, ye2)
    copies = edge_copies(1, xe2, ye2, xa, ya)
    for copy in copies:
        copy.start()
    saves = []
    for q in range(planes // GROUP):
        place_lines(q, block, high, low, frc, out)
        at = pl.ds(q * GROUP, GROUP)
        saves.append(pltpu.make_async_copy(frc.at[:, at], f_hbm.at[:, at], save.at[2 * q]))
        saves.append(pltpu.make_async_copy(out.at[:, at], out_hbm.at[:, at], save.at[2 * q + 1]))
        for copy in saves[-2:]:
            copy.start()
    for copy in copies + saves:
        copy.wait()
    visc_save.wait()


def second_kernel(n_gx, n_gy, starts, *refs):
    (f_in, vel_in, visc_in, adj_in, xh, yc, xa, ya,
     out_hbm,
     vel, visc, adj, ux, uy, uz, vv, yhs, out, frc, load, save) = refs
    planes, rows, cols = visc.shape
    ends = starts[1:] + (planes,)

    def group(g):
        here = pl.ds(starts[g], ends[g] - starts[g])
        there = pl.ds(starts[g] + 1, ends[g] - starts[g])
        return [
            pltpu.make_async_copy(vel_in.at[:, here], vel.at[:, here], load.at[0, g]),
            pltpu.make_async_copy(visc_in.at[here], visc.at[here], load.at[1, g]),
            pltpu.make_async_copy(f_in.at[:, here], frc.at[:, here], load.at[2, g]),
        ] + [
            pltpu.make_async_copy(
                adj_in.at[:, here, :, pl.ds(h * LANES, LANES)],
                adj.at[:, there, h, pl.ds(PAD, rows), :],
                load.at[3 + h, g],
            )
            for h in range(2)
        ]

    groups = [group(g) for g in range(len(starts))]
    for copies in groups:
        for copy in copies:
            copy.start()
    clear_outside(planes, rows, cols, adj, uz, vv)
    index = (n_gx, n_gy)
    set_rows(planes, rows, index, xa, xh, adj, ux, vv)
    adjoint_lanes = lane_iota(rows) < 6 * planes
    yhs[0] = jnp.where(adjoint_lanes, from_sides(ya, index), yc[0])
    yhs[1] = yc[1]

    def fields(z):
        set_fields(z, vel, visc, ux, uy, uz, vv)

    for copy in groups[0]:
        copy.wait()
    fields(0)

    @pl.loop(0, planes)
    def _(z):
        for g in range(1, len(starts)):

            @pl.when(z + 1 == starts[g])
            def _():
                for copy in groups[g]:
                    copy.wait()

        @pl.when(z + 1 < planes)
        def _():
            fields(z + 1)

        sweep_plane(z, planes, rows, adj, ux, uy, uz, vv, yhs, frc, out)
        pltpu.make_async_copy(out.at[:, z], out_hbm.at[:, z], save).start()

    pltpu.make_async_copy(out, out_hbm, save).wait()


def field_scratch(planes, rows, cols):
    f32, bf16 = jnp.float32, jnp.bfloat16
    tall = rows + 2 * PAD
    return [
        pltpu.VMEM((planes, rows, cols), bf16),
        pltpu.VMEM((3, planes + 2, 2, tall, LANES), f32),
        pltpu.VMEM((planes + 2, 2, tall, LANES), f32),
        pltpu.VMEM((planes + 2, rows, cols), f32),
        pltpu.VMEM((planes + 2, rows, cols), f32),
        pltpu.VMEM((planes + 2, 2, tall, LANES), f32),
        pltpu.VMEM((2, rows, LANES), f32),
        pltpu.VMEM((3, planes, rows, cols), f32),
        pltpu.VMEM((3, planes, rows, cols), f32),
    ]


def local(
    n_gx,
    n_gy,
    velocity,
    kinetic_energy,
    dissipation_rate,
    adjoint_start,
    interp_weight,
    observed,
    window_weight,
    window_source,
    window_block,
    window_count,
):
    planes, rows, cols = kinetic_energy.shape
    peers = n_gx * n_gy
    windows = window_block.shape[0]
    f32, bf16 = jnp.float32, jnp.bfloat16
    shape = jax.ShapeDtypeStruct
    vmem = pl.BlockSpec(memory_space=pltpu.VMEM)
    hbm = pl.BlockSpec(memory_space=pl.ANY)
    dma = pltpu.SemaphoreType.DMA
    whole = shape(adjoint_start.shape, f32)
    sides = [
        shape((2, 5 * planes, cols), f32),
        shape((2, rows, LANES), f32),
        shape((2, 3 * planes, cols), f32),
        shape((2, rows, LANES), f32),
    ]
    edges = [
        (2, 5 * planes, cols),
        (2, rows, LANES),
        (2, 2, rows, LANES),
        (2, 3 * planes, cols),
        (rows, LANES),
    ]
    flat = (1, windows)
    adjoint, forcing, visc, xh, yc, xa, ya = pl.pallas_call(
        functools.partial(first_kernel, n_gx, n_gy),
        name="route_and_first_sweep",
        in_specs=[vmem] * 6 + [hbm] * 4,
        out_specs=[hbm] * 3 + [vmem] * 4,
        out_shape=[whole, whole, shape((planes, rows, cols), bf16)] + sides,
        scratch_shapes=[
            pltpu.VMEM((peers, SUB, HALF), f32),
            pltpu.VMEM((peers, SUB, HALF), f32),
            pltpu.VMEM((3, planes, rows, cols), bf16),
            pltpu.VMEM((planes, rows, cols), bf16),
            pltpu.VMEM((planes, rows, cols), bf16),
        ]
        + field_scratch(planes, rows, cols)
        + [
            pltpu.VMEM((peers * CAP, 3 * cols), bf16),
            pltpu.VMEM((peers * CAP, 3 * cols), bf16),
        ]
        + [pltpu.VMEM(e, f32) for e in edges]
        + [dma((5,)), dma((2 * planes // GROUP + 1,)), dma, dma, dma, dma((2, 4)), dma((2, 4))],
        compiler_params=pltpu.CompilerParams(
            collective_id=0, has_side_effects=True, vmem_limit_bytes=60 << 20
        ),
    )(
        window_source.reshape(flat),
        window_block.reshape(flat),
        window_count.reshape(flat),
        window_weight.reshape(flat),
        observed,
        interp_weight,
        velocity,
        kinetic_energy,
        dissipation_rate,
        adjoint_start,
    )
    starts = (0, 1, 2, 4, 8, 12)
    return pl.pallas_call(
        functools.partial(second_kernel, n_gx, n_gy, starts),
        name="second_sweep",
        in_specs=[hbm] * 4 + [vmem] * 4,
        out_specs=hbm,
        out_shape=whole,
        scratch_shapes=[pltpu.VMEM((3, planes, rows, cols), bf16)]
        + field_scratch(planes, rows, cols)
        + [dma((5, len(starts))), dma],
        compiler_params=pltpu.CompilerParams(vmem_limit_bytes=60 << 20),
    )(forcing, velocity, visc, adjoint, xh, yc, xa, ya)


def solution(mesh):
    placed = (
        P(None, None, "gx", "gy"),
        P(None, "gx", "gy"),
        P(None, "gx", "gy"),
        P(None, None, "gx", "gy"),
        P(),
        P(None, ("gx", "gy"), None),
        P(("gx", "gy")),
        P(("gx", "gy"), None),
        P(("gx", "gy")),
        P(("gx", "gy")),
    )
    return jax.shard_map(
        functools.partial(local, mesh.shape["gx"], mesh.shape["gy"]),
        mesh=mesh,
        in_specs=placed,
        out_specs=P(None, None, "gx", "gy"),
        check_vma=False,
    )
```

```python
import functools

import jax
import jax.numpy as jnp
from jax import lax
from jax.experimental import pallas as pl
from jax.experimental.pallas import tpu as pltpu
from jax.sharding import PartitionSpec as P

MESH = pl.DeviceIdType.MESH
SWEEPS = 2
CAP = 4
LANES = 128
SUB = 8

base_viscosity = 0.05
pseudo_step = 0.4
half_step = 0.5 * pseudo_step

HALF = 2 * LANES
PLANE, ROW, COUNT, WEIGHT = 0, 1, 2, 3
PAD = 8


def lane_iota(rows=SUB):
    return lax.broadcasted_iota(jnp.int32, (rows, LANES), 1)


def split(x, pieces):
    out = []
    for _ in range(pieces):
        piece = x.astype(jnp.bfloat16)
        out.append(piece)
        x = x - piece.astype(jnp.float32)
    return out


def fill_slots(source, block, count, weight, obs_ref, slots_ref, rows):
    windows = source.shape[1]
    peers = slots_ref.shape[0]
    slots = peers * CAP
    f32 = jnp.float32
    meta = [block // rows, block % rows, count] + split(weight, 3) + [source]
    meta = [row.astype(f32) for row in meta]
    meta = jnp.concatenate(meta + [jnp.zeros((LANES - len(meta), windows), f32)], axis=0).T
    first = lax.broadcasted_iota(jnp.int32, (windows, windows), 0)
    second = lax.broadcasted_iota(jnp.int32, (windows, windows), 1)
    same = (meta[:, 6:7] == source.astype(f32)) & (first < second)
    place = jnp.sum(same.astype(f32), axis=0, keepdims=True).astype(jnp.int32)
    chosen = lax.broadcasted_iota(jnp.int32, (slots, windows), 0) == source * CAP + place
    chosen = chosen.astype(jnp.bfloat16)
    top = lax.broadcasted_iota(jnp.int32, (slots // SUB, SUB, LANES), 1) < CAP
    quarters = []
    for values in (obs_ref[0], obs_ref[1], obs_ref[2], meta):
        total = jnp.dot(chosen, values.astype(jnp.bfloat16), preferred_element_type=f32)
        quarters.append(total.reshape(slots // SUB, SUB, LANES))
    for h in range(2):
        upper, lower = quarters[h], quarters[2 + h]
        even = jnp.where(top, upper, pltpu.roll(lower, CAP, axis=1))
        odd = jnp.where(top, pltpu.roll(upper, CAP, axis=1), lower)
        both = jnp.stack([even, odd], axis=1).reshape(peers, SUB, LANES)
        slots_ref[:, :, h * LANES : (h + 1) * LANES] = both.astype(jnp.bfloat16)


def read_slots(recv_ref):
    peers = recv_ref.shape[0]
    top = lax.broadcasted_iota(jnp.int32, (peers // 2, SUB, LANES), 1) < CAP
    quarters = [None] * 4
    for h in range(2):
        half = recv_ref[:, :, h * LANES : (h + 1) * LANES].astype(jnp.float32)
        pairs = half.reshape(peers // 2, 2, SUB, LANES)
        even, odd = pairs[:, 0], pairs[:, 1]
        upper = jnp.where(top, even, pltpu.roll(odd, CAP, axis=1))
        lower = jnp.where(top, pltpu.roll(even, CAP, axis=1), odd)
        quarters[h] = upper.reshape(peers * CAP, LANES)
        quarters[2 + h] = lower.reshape(peers * CAP, LANES)
    return quarters


def line_forcing(quarters, vel_ref, weight_ref, high_ref, low_ref):
    meta = quarters[3]
    slots = meta.shape[0]
    planes, rows, cols = vel_ref.shape[1:]
    weights = weight_ref[...]
    block = (meta[:, PLANE : PLANE + 1] * rows + meta[:, ROW : ROW + 1]).astype(jnp.int32)
    count = meta[:, COUNT : COUNT + 1].astype(jnp.int32)
    scale = sum(meta[:, WEIGHT + k : WEIGHT + k + 1] for k in (2, 1, 0))
    inside = lax.broadcasted_iota(jnp.int32, (slots, cols), 1) < count
    group = 4
    lines = [jnp.zeros((slots, cols), jnp.float32) for _ in range(3)]
    for q in range(planes // group):
        number = lax.broadcasted_iota(jnp.int32, (slots, group * rows), 1) + q * group * rows
        chosen = (number == block).astype(jnp.bfloat16)
        for c in range(3):
            some = vel_ref[c, q * group : (q + 1) * group].reshape(group * rows, cols)
            lines[c] = lines[c] + jnp.dot(chosen, some, preferred_element_type=jnp.float32)
    edge_values = []
    for c in range(3):
        masked = jnp.where(inside, lines[c], 0.0).astype(jnp.bfloat16)
        predicted = lax.dot_general(
            masked, weights, (((1,), (1,)), ((), ())), preferred_element_type=jnp.float32
        )
        high, low = split(scale * (predicted - quarters[c]), 2)
        placed = jnp.dot(low, weights, preferred_element_type=jnp.float32)
        placed = placed + jnp.dot(high, weights, preferred_element_type=jnp.float32)
        placed = jnp.where(inside, pseudo_step * placed, 0.0)
        edge_values.append((placed[:, 0:1], placed[:, cols - 1 : cols]))
        high, low = split(placed, 2)
        high_ref[:, c * cols : (c + 1) * cols] = high
        low_ref[:, c * cols : (c + 1) * cols] = low
    return edge_values


def force_edges(block, meta, edge_values, high_ref, low_ref, planes, rows, xe, ye):
    f32, bf16 = jnp.float32, jnp.bfloat16
    slots, width = high_ref.shape
    cols = width // 3
    number = lax.broadcasted_iota(jnp.int32, (2 * planes, slots), 0)
    line = number % planes * rows + number // planes * (rows - 1)
    chosen = (line == block).astype(bf16)
    total = jnp.dot(chosen, low_ref[...], preferred_element_type=f32)
    total = total + jnp.dot(chosen, high_ref[...], preferred_element_type=f32)
    for side in range(2):
        for c in range(3):
            at = slice(c * planes, (c + 1) * planes)
            xe[side, at, :] = xe[side, at, :] + total[side * planes : (side + 1) * planes, c * cols : (c + 1) * cols]
    lanes = lane_iota(slots)
    plane = meta[:, PLANE : PLANE + 1].astype(jnp.int32)
    values = jnp.zeros((slots, LANES), f32)
    for c in range(3):
        for side in range(2):
            values = jnp.where(lanes // (2 * planes) * 2 + (1 - lanes % 2) == 2 * c + side, edge_values[c][side], values)
    values = jnp.where((lanes // 2 % planes == plane) & (lanes < 6 * planes), values, 0.0)
    chosen = (lax.broadcasted_iota(jnp.int32, (rows, slots), 0) == block % rows).astype(bf16)
    total = ye[...]
    for piece in reversed(split(values, 2)):
        total = total + jnp.dot(chosen, piece, preferred_element_type=f32)
    ye[...] = total


GROUP = 4


def place_lines(q, block, high_ref, low_ref, forcing, out):
    slots = high_ref.shape[0]
    rows, cols = forcing.shape[2:]
    step = GROUP * rows
    number = lax.broadcasted_iota(jnp.int32, (step, slots), 0) + q * step
    chosen = (number == block).astype(jnp.bfloat16)
    at = slice(q * GROUP, (q + 1) * GROUP)
    for c in range(3):
        lanes = slice(c * cols, (c + 1) * cols)
        total = jnp.dot(chosen, low_ref[:, lanes], preferred_element_type=jnp.float32)
        total = total + jnp.dot(chosen, high_ref[:, lanes], preferred_element_type=jnp.float32)
        total = total.reshape(GROUP, rows, cols)
        forcing[c, at] = total
        out[c, at] = out[c, at] + total


def pack_rows(fields, rows, cols, xe):
    for k, read in enumerate(fields):
        for h in range(2):
            half = slice(h * LANES, (h + 1) * LANES)
            xe[0, k : k + 1, half] = read(slice(0, 1), h)
            xe[1, k : k + 1, half] = read(slice(rows - 1, rows), h)


def pack_columns(fields, rows, ye):
    lanes = lane_iota()

    @pl.loop(0, rows // SUB)
    def _(r):
        at = pl.ds(pl.multiple_of(r * SUB, SUB), SUB)
        packed = jnp.zeros((SUB, LANES), jnp.float32)
        for k, read in fields:
            ends = jnp.where(lanes == 0, read(at, 0), read(at, 1))
            ends = pltpu.roll(ends, (2 * k + 1) % LANES, axis=1)
            packed = jnp.where(lanes // 2 == k, ends, packed)
        ye[at, :] = packed


def scaled_from(shape, axis, first, factor):
    return jnp.where(lax.broadcasted_iota(jnp.int32, shape, axis) < first, 1.0, factor)


def from_sides(below, above, index):
    inner = inside_flags(*index)
    odd = lane_iota(below.shape[0]) % 2 == 1
    below, above = below * inner[2], above * inner[3]
    moved = jnp.where(odd, pltpu.roll(below, 1, axis=1), pltpu.roll(above, LANES - 1, axis=1))
    return moved, jnp.where(odd, below, above)


def inside_flags(n_gx, n_gy):
    gx, gy = lax.axis_index("gx"), lax.axis_index("gy")
    flags = (gx > 0, gx < n_gx - 1, gy > 0, gy < n_gy - 1)
    return [flag.astype(jnp.float32) for flag in flags]


def shifted(rows, by):
    if isinstance(rows, slice):
        return slice(rows.start + by, rows.stop + by)
    return pl.ds(pl.multiple_of(rows.start + by, SUB), rows.size)


def clear_outside(planes, rows, cols, adj, uz, vv):
    zero = jnp.zeros((rows, cols), jnp.float32)
    for at in (0, planes + 1):
        uz[at] = zero
        for h in range(2):
            vv[at, h, PAD : PAD + rows, :] = zero[:, :LANES]
            for c in range(3):
                adj[c, at, h, PAD : PAD + rows, :] = zero[:, :LANES]


def set_fields(z, vel, visc, ux, uy, uz, vv):
    rows = visc.shape[1]
    uy[z + 1] = vel[1, z].astype(jnp.float32) * half_step
    uz[z + 1] = vel[2, z].astype(jnp.float32) * half_step
    for h in range(2):
        half = slice(h * LANES, (h + 1) * LANES)
        vv[z + 1, h, PAD : PAD + rows, :] = visc[z, :, half].astype(jnp.float32) * half_step
        ux[z + 1, h, PAD : PAD + rows, :] = vel[0, z, :, half].astype(jnp.float32) * half_step


def clear_rows(planes, rows, adj, ux, vv):
    zero = jnp.zeros((PAD, LANES), jnp.float32)
    for at in (0, PAD + rows):
        for z in range(planes):
            for h in range(2):
                for ref in (ux, vv):
                    ref[z + 1, h, at : at + PAD, :] = zero
                for c in range(3):
                    adj[c, z + 1, h, at : at + PAD, :] = zero


def add_rows(planes, rows, xe, xh, out):
    for side, at, sign in ((0, 0, 1.0), (1, rows - 1, -1.0)):
        v_out = xh[side, 4 * planes : 5 * planes, :]
        coef = xe[side, 4 * planes : 5 * planes, :] + v_out + sign * xh[side, 3 * planes : 4 * planes, :]
        for c in range(3):
            mine = slice(c * planes, (c + 1) * planes)
            share = coef * xh[side, mine, :] - v_out * xe[side, mine, :]
            for z in range(planes):
                out[c, z, at : at + 1, :] = out[c, z, at : at + 1, :] + share[z : z + 1, :]


def column_fix(planes, own, outside, normal):
    lanes = lane_iota(own.shape[0])
    coef = own + outside + jnp.where(lanes % 2 == 1, normal, -normal)

    def spread(x):
        for_c = [pltpu.roll(x, LANES - 2 * planes * (3 - c), axis=1) for c in range(3)]
        return jnp.where(lanes < 2 * planes, for_c[0], jnp.where(lanes < 4 * planes, for_c[1], for_c[2]))

    share = spread(coef) * outside - spread(outside) * own
    return jnp.where(lanes < 6 * planes, share, 0.0)


def add_columns(planes, rows, fix, out):
    lanes = lane_iota()

    @pl.loop(0, rows // SUB)
    def _(r):
        at = pl.ds(pl.multiple_of(r * SUB, SUB), SUB)
        packed = fix[at, :]
        for k in range(3 * planes):
            c, z = k // planes, k % planes
            moved = pltpu.roll(packed, LANES - 1 - 2 * k, axis=1)
            left, right = slice(0, LANES), slice(LANES, 2 * LANES)
            out[c, z, at, left] = out[c, z, at, left] + jnp.where(lanes == 0, moved, 0.0)
            out[c, z, at, right] = out[c, z, at, right] + jnp.where(lanes == LANES - 1, moved, 0.0)


def set_rows(planes, rows, xa, xh, adj, ux, vv):
    for side, at in ((0, PAD - 1), (1, PAD + rows)):
        for z in range(planes):
            for h in range(2):
                half = slice(h * LANES, (h + 1) * LANES)
                for c in range(3):
                    k = c * planes + z
                    adj[c, z + 1, h, at : at + 1, :] = xa[side, k : k + 1, half]
                k = 3 * planes + z
                ux[z + 1, h, at : at + 1, :] = xh[side, k : k + 1, half]
                k = 4 * planes + z
                vv[z + 1, h, at : at + 1, :] = xh[side, k : k + 1, half]


def up_down(pair, outer, first, last):
    left, right = pair
    left_up, right_up = (pltpu.roll(x, LANES - 1, axis=1) for x in pair)
    left_down, right_down = (pltpu.roll(x, 1, axis=1) for x in pair)
    up = (jnp.where(last, right_up, left_up), jnp.where(last, outer, right_up))
    down = (jnp.where(first, outer, left_down), jnp.where(first, left_down, right_down))
    return up, down


def sweep_plane(z, planes, rows, adj, ux, uy, uz, vv, yhs, forcing, out):
    lanes = lane_iota()
    first, last = lanes == 0, lanes == LANES - 1
    here = z + 1
    both = (slice(0, LANES), slice(LANES, 2 * LANES))

    for r in range(rows // SUB):
        at = slice(r * SUB, (r + 1) * SUB)
        mid, plus, minus = (slice(at.start + PAD + d, at.stop + PAD + d) for d in (0, 1, -1))
        edges = [yhs[0, at, :], yhs[1, at, :]]

        def outer(which, k):
            return pltpu.roll(edges[which], LANES - 1 - 2 * (k * planes + z), axis=1)

        v = [vv[here, h, mid, :] for h in range(2)]
        v_yp, v_ym = up_down(v, outer(0, 3), first, last)
        u_yp, u_ym = up_down([uy[here, at, half] for half in both], outer(1, 3), first, last)
        coef = []
        for h in range(2):
            n_xp, n_xm = v[h] + vv[here, h, plus, :], v[h] + vv[here, h, minus, :]
            n_yp, n_ym = v[h] + v_yp[h], v[h] + v_ym[h]
            n_zp, n_zm = v[h] + vv[here + 1, h, mid, :], v[h] + vv[here - 1, h, mid, :]
            coef.append(
                (
                    1.0 - ((n_xp + n_xm) + (n_yp + n_ym) + (n_zp + n_zm)),
                    n_xp - ux[here, h, plus, :],
                    n_xm + ux[here, h, minus, :],
                    n_yp - u_yp[h],
                    n_ym + u_ym[h],
                    n_zp - uz[here + 1, at, both[h]],
                    n_zm + uz[here - 1, at, both[h]],
                )
            )
        for c in range(3):
            a = [adj[c, here, h, mid, :] for h in range(2)]
            a_yp, a_ym = up_down(a, outer(0, c), first, last)
            for h in range(2):
                k = coef[h]
                value = k[0] * a[h] + (k[1] * adj[c, here, h, plus, :] + k[2] * adj[c, here, h, minus, :])
                value = value + (k[3] * a_yp[h] + k[4] * a_ym[h])
                value = value + (k[5] * adj[c, here + 1, h, mid, :] + k[6] * adj[c, here - 1, h, mid, :])
                if forcing is not None:
                    value = value + forcing[c, z, at, both[h]]
                out[c, z, at, both[h]] = value


def first_kernel(n_gx, n_gy, *refs):
    (source, block, count, weight, obs_in, weights_in, vel_in, ke_in, dr_in, adj_in,
     out_hbm, f_hbm, visc_hbm, xh_hbm, yc_hbm, xa, ya,
     slots, recv, obs, weights, vel, ke, dr, visc, adj, ux, uy, uz, vv, yhs, out, frc, high, low, xe, xh, ye, xe2, ye2, yfix,
     x_out, x_in, y_out, y_in, x_out2, y_out2,
     load, save, all_send, all_recv, local_sem, send, received) = refs
    planes, rows, cols = visc.shape
    peers = n_gx * n_gy
    gx, gy = lax.axis_index("gx"), lax.axis_index("gy")
    me = gx * n_gy + gy

    def device(step):
        peer = lax.rem(me + step, peers)
        return peer, (peer // n_gy, lax.rem(peer, n_gy))

    lower_x = (lax.rem(gx + n_gx - 1, n_gx), gy)
    upper_x = (lax.rem(gx + 1, n_gx), gy)
    lower_y = (gx, lax.rem(gy + n_gy - 1, n_gy))
    upper_y = (gx, lax.rem(gy + 1, n_gy))

    def edge_copies(turn, x_from, y_from, x_to, y_to):
        sides = (
            (x_from.at[1], x_to.at[0], upper_x),
            (x_from.at[0], x_to.at[1], lower_x),
            (y_from[1], y_to.at[0], upper_y),
            (y_from[0], y_to.at[1], lower_y),
        )
        return [
            pltpu.make_async_remote_copy(
                here, there, send.at[turn, k], received.at[turn, k], device_id=where, device_id_type=MESH
            )
            for k, (here, there, where) in enumerate(sides)
        ]

    loads = [
        pltpu.make_async_copy(ke_in, ke, load.at[0]),
        pltpu.make_async_copy(dr_in, dr, load.at[1]),
        pltpu.make_async_copy(vel_in, vel, load.at[2]),
    ] + [
        pltpu.make_async_copy(
            adj_in.at[:, :, :, pl.ds(h * LANES, LANES)],
            adj.at[:, pl.ds(1, planes), h, pl.ds(PAD, rows), :],
            load.at[3 + h],
        )
        for h in range(2)
    ]
    ahead = [
        pltpu.make_async_copy(obs_in, obs, load.at[5]),
        pltpu.make_async_copy(weights_in, weights, load.at[6]),
    ]
    for copy in ahead + loads:
        copy.start()
    barrier = pltpu.get_barrier_semaphore()

    @pl.loop(1, peers)
    def _(step):
        pl.semaphore_signal(barrier, inc=1, device_id=device(step)[1], device_id_type=MESH)

    for copy in ahead:
        copy.wait()
    fill_slots(source[...], block[...], count[...], weight[...], obs, slots, rows)
    clear_outside(planes, rows, cols, adj, uz, vv)
    for copy in loads[:3]:
        copy.wait()

    @pl.loop(0, planes)
    def _(z):
        value = base_viscosity + ke[z].astype(jnp.float32) / dr[z].astype(jnp.float32)
        visc[z] = value.astype(jnp.bfloat16)
        set_fields(z, vel, visc, ux, uy, uz, vv)

    visc_save = pltpu.make_async_copy(visc, visc_hbm, save.at[8])
    visc_save.start()
    for copy in loads[3:]:
        copy.wait()

    def of_adj(c, z):
        return lambda at, h: adj[c, z + 1, h, shifted(at, PAD), :]

    def of_tall(ref, z):
        return lambda at, h: ref[z + 1, h, shifted(at, PAD), :]

    def of_uy(z):
        return lambda at, h: uy[z + 1, at, slice(h * LANES, (h + 1) * LANES)]

    starts = [of_adj(c, z) for c in range(3) for z in range(planes)]
    visc_fields = [of_tall(vv, z) for z in range(planes)]
    pack_rows(starts + [of_tall(ux, z) for z in range(planes)] + visc_fields, rows, cols, xe)
    pack_columns(list(enumerate(starts + visc_fields)), rows, ye.at[0])
    pack_columns([(3 * planes + z, of_uy(z)) for z in range(planes)], rows, ye.at[1])

    bf16, f32 = jnp.bfloat16, jnp.float32
    unscale_rows = scaled_from(xe.shape[1:], 0, 3 * planes, 1.0 / half_step)
    unscale_lanes = scaled_from((rows, LANES), 1, 6 * planes, 1.0 / half_step)
    for side in range(2):
        x_out[side] = (xe[side] * unscale_rows).astype(bf16)
    odd = lane_iota(rows) % 2 == 1
    main, normal = ye[0] * unscale_lanes, ye[1] * unscale_lanes
    y_out[0] = jnp.where(odd, main, pltpu.roll(normal, LANES - 1, axis=1)).astype(bf16)
    y_out[1] = jnp.where(odd, pltpu.roll(normal, 1, axis=1), main).astype(bf16)

    pl.semaphore_wait(barrier, peers - 1)
    copies = edge_copies(0, x_out, (y_out.at[0], y_out.at[1]), x_in, y_in)
    for copy in copies:
        copy.start()
    own = pltpu.make_async_copy(slots.at[me], recv.at[me], local_sem)
    own.start()

    def send_slots(step):
        peer, where = device(step)
        pltpu.make_async_remote_copy(
            slots.at[peer], recv.at[me], all_send, all_recv, device_id=where, device_id_type=MESH
        ).start()

    pl.loop(1, peers)(send_slots)

    clear_rows(planes, rows, adj, ux, vv)
    yhs[...] = jnp.zeros_like(yhs)

    @pl.loop(0, planes)
    def _(z):
        sweep_plane(z, planes, rows, adj, ux, uy, uz, vv, yhs, None, out)

    for copy in copies:
        copy.wait()
    index = (n_gx, n_gy)
    inner = inside_flags(*index)
    scale_rows = scaled_from(xe.shape[1:], 0, 3 * planes, half_step)
    scale_lanes = scaled_from((rows, LANES), 1, 6 * planes, half_step)
    for side in range(2):
        xh[side] = x_in[side].astype(f32) * (scale_rows * inner[side])
    below, above = (y_in[side].astype(f32) * scale_lanes for side in range(2))
    yhs[0], yhs[1] = from_sides(below, above, index)
    side_saves = [
        pltpu.make_async_copy(xh, xh_hbm, save.at[9]),
        pltpu.make_async_copy(yhs, yc_hbm, save.at[10]),
    ]
    for copy in side_saves:
        copy.start()
    add_rows(planes, rows, xe, xh, out)
    fix = column_fix(planes, ye[0], yhs[0], yhs[1])
    yfix[...] = fix

    def of_out(c, z):
        return lambda at, h: out[c, z, at, slice(h * LANES, (h + 1) * LANES)]

    news = [of_out(c, z) for c in range(3) for z in range(planes)]
    pack_rows(news, rows, cols, xe2)
    pack_columns(list(enumerate(news)), rows, ye2)
    ye2[...] = ye2[...] + fix
    for side, at in ((0, 0), (1, rows - 1)):
        row = jnp.broadcast_to(fix[at : at + 1], (3 * planes, LANES))
        spot = lax.broadcasted_iota(jnp.int32, row.shape, 1)
        field = 2 * lax.broadcasted_iota(jnp.int32, row.shape, 0)
        for which, lane, half in ((1, 0, slice(0, LANES)), (0, LANES - 1, slice(LANES, 2 * LANES))):
            corner = jnp.sum(jnp.where(spot == field + which, row, 0.0), axis=1, keepdims=True)
            xe2[side, :, half] = xe2[side, :, half] + jnp.where(spot == lane, corner, 0.0)

    own.wait()
    rest = pl.ds(0, peers - 1)
    pltpu.make_async_copy(slots.at[rest], slots.at[rest], all_send).wait()
    pltpu.make_async_copy(recv.at[rest], recv.at[rest], all_recv).wait()
    quarters = read_slots(recv)
    edge_values = line_forcing(quarters, vel, weights, high, low)
    across = quarters[3].T
    block = (across[PLANE : PLANE + 1] * rows + across[ROW : ROW + 1]).astype(jnp.int32)
    force_edges(block, quarters[3], edge_values, high, low, planes, rows, xe2, ye2)
    x_out2[...] = xe2[...].astype(bf16)
    y_out2[...] = ye2[...].astype(bf16)
    copies = edge_copies(1, x_out2, (y_out2, y_out2), xa, ya)
    for copy in copies:
        copy.start()
    add_columns(planes, rows, yfix, out)
    saves = []
    for q in range(planes // GROUP):
        place_lines(q, block, high, low, frc, out)
        at = pl.ds(q * GROUP, GROUP)
        saves.append(pltpu.make_async_copy(frc.at[:, at], f_hbm.at[:, at], save.at[2 * q]))
        saves.append(pltpu.make_async_copy(out.at[:, at], out_hbm.at[:, at], save.at[2 * q + 1]))
        for copy in saves[-2:]:
            copy.start()
    for copy in copies + saves + side_saves:
        copy.wait()
    visc_save.wait()


def second_kernel(n_gx, n_gy, starts, *refs):
    (f_in, vel_in, visc_in, adj_in, xh_in, yc_in, xa_in, ya_in,
     out_hbm,
     vel, visc, adj, ux, uy, uz, vv, yhs, out, frc, xh, yc, x_in, y_in, xa, load, save) = refs
    planes, rows, cols = visc.shape
    ends = starts[1:] + (planes,)

    def group(g):
        here = pl.ds(starts[g], ends[g] - starts[g])
        there = pl.ds(starts[g] + 1, ends[g] - starts[g])
        return [
            pltpu.make_async_copy(vel_in.at[:, here], vel.at[:, here], load.at[0, g]),
            pltpu.make_async_copy(visc_in.at[here], visc.at[here], load.at[1, g]),
            pltpu.make_async_copy(f_in.at[:, here], frc.at[:, here], load.at[2, g]),
        ] + [
            pltpu.make_async_copy(
                adj_in.at[:, here, :, pl.ds(h * LANES, LANES)],
                adj.at[:, there, h, pl.ds(PAD, rows), :],
                load.at[3 + h, g],
            )
            for h in range(2)
        ]

    groups = [group(g) for g in range(len(starts))]
    sides = [
        pltpu.make_async_copy(a, b, load.at[5, k])
        for k, (a, b) in enumerate(((xh_in, xh), (xa_in, x_in), (yc_in, yc), (ya_in, y_in)))
    ]
    for copies in [sides] + groups:
        for copy in copies:
            copy.start()
    clear_outside(planes, rows, cols, adj, uz, vv)
    for copy in sides:
        copy.wait()
    index = (n_gx, n_gy)
    inner = inside_flags(*index)
    for side in range(2):
        xa[side] = x_in[side].astype(jnp.float32) * inner[side]
    set_rows(planes, rows, xa, xh, adj, ux, vv)
    below, above = (y_in[side].astype(jnp.float32) for side in range(2))
    adjoint_lanes = lane_iota(rows) < 6 * planes
    yhs[0] = jnp.where(adjoint_lanes, from_sides(below, above, index)[0], yc[0])
    yhs[1] = yc[1]

    def fields(z):
        set_fields(z, vel, visc, ux, uy, uz, vv)

    for copy in groups[0]:
        copy.wait()
    fields(0)

    @pl.loop(0, planes)
    def _(z):
        for g in range(1, len(starts)):

            @pl.when(z + 1 == starts[g])
            def _():
                for copy in groups[g]:
                    copy.wait()

        @pl.when(z + 1 < planes)
        def _():
            fields(z + 1)

        sweep_plane(z, planes, rows, adj, ux, uy, uz, vv, yhs, frc, out)
        pltpu.make_async_copy(out.at[:, z], out_hbm.at[:, z], save).start()

    pltpu.make_async_copy(out, out_hbm, save).wait()


def field_scratch(planes, rows, cols):
    f32, bf16 = jnp.float32, jnp.bfloat16
    tall = rows + 2 * PAD
    return [
        pltpu.VMEM((planes, rows, cols), bf16),
        pltpu.VMEM((3, planes + 2, 2, tall, LANES), f32),
        pltpu.VMEM((planes + 2, 2, tall, LANES), f32),
        pltpu.VMEM((planes + 2, rows, cols), f32),
        pltpu.VMEM((planes + 2, rows, cols), f32),
        pltpu.VMEM((planes + 2, 2, tall, LANES), f32),
        pltpu.VMEM((2, rows, LANES), f32),
        pltpu.VMEM((3, planes, rows, cols), f32),
        pltpu.VMEM((3, planes, rows, cols), f32),
    ]


def local(
    n_gx,
    n_gy,
    velocity,
    kinetic_energy,
    dissipation_rate,
    adjoint_start,
    interp_weight,
    observed,
    window_weight,
    window_source,
    window_block,
    window_count,
):
    planes, rows, cols = kinetic_energy.shape
    peers = n_gx * n_gy
    windows = window_block.shape[0]
    f32, bf16 = jnp.float32, jnp.bfloat16
    shape = jax.ShapeDtypeStruct
    vmem = pl.BlockSpec(memory_space=pltpu.VMEM)
    hbm = pl.BlockSpec(memory_space=pl.ANY)
    dma = pltpu.SemaphoreType.DMA
    whole = shape(adjoint_start.shape, f32)
    sides = [
        shape((2, 5 * planes, cols), f32),
        shape((2, rows, LANES), f32),
        shape((2, 3 * planes, cols), bf16),
        shape((2, rows, LANES), bf16),
    ]
    edges = [
        (2, 5 * planes, cols),
        (2, 5 * planes, cols),
        (2, rows, LANES),
        (2, 3 * planes, cols),
        (rows, LANES),
        (rows, LANES),
    ]
    messages = [
        (2, 5 * planes, cols),
        (2, 5 * planes, cols),
        (2, rows, LANES),
        (2, rows, LANES),
        (2, 3 * planes, cols),
        (rows, LANES),
    ]
    flat = (1, windows)
    adjoint, forcing, visc, xh, yc, xa, ya = pl.pallas_call(
        functools.partial(first_kernel, n_gx, n_gy),
        name="route_and_first_sweep",
        in_specs=[vmem] * 4 + [hbm] * 6,
        out_specs=[hbm] * 7,
        out_shape=[whole, whole, shape((planes, rows, cols), bf16)] + sides,
        scratch_shapes=[
            pltpu.VMEM((peers, SUB, HALF), bf16),
            pltpu.VMEM((peers, SUB, HALF), bf16),
            pltpu.VMEM(observed.shape, f32),
            pltpu.VMEM(interp_weight.shape, bf16),
            pltpu.VMEM((3, planes, rows, cols), bf16),
            pltpu.VMEM((planes, rows, cols), bf16),
            pltpu.VMEM((planes, rows, cols), bf16),
        ]
        + field_scratch(planes, rows, cols)
        + [
            pltpu.VMEM((peers * CAP, 3 * cols), bf16),
            pltpu.VMEM((peers * CAP, 3 * cols), bf16),
        ]
        + [pltpu.VMEM(e, f32) for e in edges] + [pltpu.VMEM(e, bf16) for e in messages]
        + [dma((7,)), dma((2 * planes // GROUP + 3,)), dma, dma, dma, dma((2, 4)), dma((2, 4))],
        compiler_params=pltpu.CompilerParams(
            collective_id=0, has_side_effects=True, vmem_limit_bytes=60 << 20
        ),
    )(
        window_source.reshape(flat),
        window_block.reshape(flat),
        window_count.reshape(flat),
        window_weight.reshape(flat),
        observed,
        interp_weight,
        velocity,
        kinetic_energy,
        dissipation_rate,
        adjoint_start,
    )
    starts = (0, 1, 2, 4, 8, 12)
    return pl.pallas_call(
        functools.partial(second_kernel, n_gx, n_gy, starts),
        name="second_sweep",
        in_specs=[hbm] * 8,
        out_specs=hbm,
        out_shape=whole,
        scratch_shapes=[pltpu.VMEM((3, planes, rows, cols), bf16)]
        + field_scratch(planes, rows, cols)
        + [pltpu.VMEM(side.shape, side.dtype) for side in sides]
        + [pltpu.VMEM(sides[2].shape, f32)]
        + [dma((6, len(starts))), dma],
        compiler_params=pltpu.CompilerParams(vmem_limit_bytes=60 << 20),
    )(forcing, velocity, visc, adjoint, xh, yc, xa, ya)


def solution(mesh):
    placed = (
        P(None, None, "gx", "gy"),
        P(None, "gx", "gy"),
        P(None, "gx", "gy"),
        P(None, None, "gx", "gy"),
        P(),
        P(None, ("gx", "gy"), None),
        P(("gx", "gy")),
        P(("gx", "gy"), None),
        P(("gx", "gy")),
        P(("gx", "gy")),
    )
    return jax.shard_map(
        functools.partial(local, mesh.shape["gx"], mesh.shape["gy"]),
        mesh=mesh,
        in_specs=placed,
        out_specs=P(None, None, "gx", "gy"),
        check_vma=False,
    )
```

```python
import functools

import jax
import jax.numpy as jnp
from jax import lax
from jax.experimental import pallas as pl
from jax.experimental.pallas import tpu as pltpu
from jax.sharding import PartitionSpec as P

MESH = pl.DeviceIdType.MESH
SWEEPS = 2
CAP = 4
LANES = 128
SUB = 8

base_viscosity = 0.05
pseudo_step = 0.4
half_step = 0.5 * pseudo_step

HALF = 2 * LANES
PLANE, ROW, COUNT, WEIGHT = 0, 1, 2, 3
PAD = 8


def lane_iota(rows=SUB):
    return lax.broadcasted_iota(jnp.int32, (rows, LANES), 1)


def split(x, pieces):
    out = []
    for _ in range(pieces):
        piece = x.astype(jnp.bfloat16)
        out.append(piece)
        x = x - piece.astype(jnp.float32)
    return out


def fill_slots(source, block, count, weight, obs_ref, slots_ref, rows):
    windows = source.shape[1]
    peers = slots_ref.shape[0]
    slots = peers * CAP
    f32 = jnp.float32
    meta = [block // rows, block % rows, count] + split(weight, 3) + [source]
    meta = [row.astype(f32) for row in meta]
    meta = jnp.concatenate(meta + [jnp.zeros((LANES - len(meta), windows), f32)], axis=0).T
    first = lax.broadcasted_iota(jnp.int32, (windows, windows), 0)
    second = lax.broadcasted_iota(jnp.int32, (windows, windows), 1)
    same = (meta[:, 6:7] == source.astype(f32)) & (first < second)
    place = jnp.sum(same.astype(f32), axis=0, keepdims=True).astype(jnp.int32)
    chosen = lax.broadcasted_iota(jnp.int32, (slots, windows), 0) == source * CAP + place
    chosen = chosen.astype(jnp.bfloat16)
    top = lax.broadcasted_iota(jnp.int32, (slots // SUB, SUB, LANES), 1) < CAP
    quarters = []
    for values in (obs_ref[0], obs_ref[1], obs_ref[2], meta):
        total = jnp.dot(chosen, values.astype(jnp.bfloat16), preferred_element_type=f32)
        quarters.append(total.reshape(slots // SUB, SUB, LANES))
    for h in range(2):
        upper, lower = quarters[h], quarters[2 + h]
        even = jnp.where(top, upper, pltpu.roll(lower, CAP, axis=1))
        odd = jnp.where(top, pltpu.roll(upper, CAP, axis=1), lower)
        both = jnp.stack([even, odd], axis=1).reshape(peers, SUB, LANES)
        slots_ref[:, :, h * LANES : (h + 1) * LANES] = both.astype(jnp.bfloat16)


def read_slots(recv_ref):
    peers = recv_ref.shape[0]
    top = lax.broadcasted_iota(jnp.int32, (peers // 2, SUB, LANES), 1) < CAP
    quarters = [None] * 4
    for h in range(2):
        half = recv_ref[:, :, h * LANES : (h + 1) * LANES].astype(jnp.float32)
        pairs = half.reshape(peers // 2, 2, SUB, LANES)
        even, odd = pairs[:, 0], pairs[:, 1]
        upper = jnp.where(top, even, pltpu.roll(odd, CAP, axis=1))
        lower = jnp.where(top, pltpu.roll(even, CAP, axis=1), odd)
        quarters[h] = upper.reshape(peers * CAP, LANES)
        quarters[2 + h] = lower.reshape(peers * CAP, LANES)
    return quarters


def line_forcing(quarters, vel_ref, weight_ref, high_ref, low_ref):
    meta = quarters[3]
    slots = meta.shape[0]
    planes, rows, cols = vel_ref.shape[1:]
    weights = weight_ref[...]
    block = (meta[:, PLANE : PLANE + 1] * rows + meta[:, ROW : ROW + 1]).astype(jnp.int32)
    count = meta[:, COUNT : COUNT + 1].astype(jnp.int32)
    scale = sum(meta[:, WEIGHT + k : WEIGHT + k + 1] for k in (2, 1, 0))
    inside = lax.broadcasted_iota(jnp.int32, (slots, cols), 1) < count
    group = 4
    lines = [jnp.zeros((slots, cols), jnp.float32) for _ in range(3)]
    for q in range(planes // group):
        number = lax.broadcasted_iota(jnp.int32, (slots, group * rows), 1) + q * group * rows
        chosen = (number == block).astype(jnp.bfloat16)
        for c in range(3):
            some = vel_ref[c, q * group : (q + 1) * group].reshape(group * rows, cols)
            lines[c] = lines[c] + jnp.dot(chosen, some, preferred_element_type=jnp.float32)
    edge_values = []
    for c in range(3):
        masked = jnp.where(inside, lines[c], 0.0).astype(jnp.bfloat16)
        predicted = lax.dot_general(
            masked, weights, (((1,), (1,)), ((), ())), preferred_element_type=jnp.float32
        )
        high, low = split(scale * (predicted - quarters[c]), 2)
        placed = jnp.dot(low, weights, preferred_element_type=jnp.float32)
        placed = placed + jnp.dot(high, weights, preferred_element_type=jnp.float32)
        placed = jnp.where(inside, pseudo_step * placed, 0.0)
        edge_values.append((placed[:, 0:1], placed[:, cols - 1 : cols]))
        high, low = split(placed, 2)
        high_ref[:, c * cols : (c + 1) * cols] = high
        low_ref[:, c * cols : (c + 1) * cols] = low
    return edge_values


def force_edges(block, meta, edge_values, high_ref, low_ref, planes, rows, xe, ye):
    f32, bf16 = jnp.float32, jnp.bfloat16
    slots, width = high_ref.shape
    cols = width // 3
    number = lax.broadcasted_iota(jnp.int32, (2 * planes, slots), 0)
    line = number % planes * rows + number // planes * (rows - 1)
    chosen = (line == block).astype(bf16)
    total = jnp.dot(chosen, low_ref[...], preferred_element_type=f32)
    total = total + jnp.dot(chosen, high_ref[...], preferred_element_type=f32)
    for side in range(2):
        for c in range(3):
            at = slice(c * planes, (c + 1) * planes)
            xe[side, at, :] = xe[side, at, :] + total[side * planes : (side + 1) * planes, c * cols : (c + 1) * cols]
    lanes = lane_iota(slots)
    plane = meta[:, PLANE : PLANE + 1].astype(jnp.int32)
    values = jnp.zeros((slots, LANES), f32)
    for c in range(3):
        for side in range(2):
            values = jnp.where(lanes // (2 * planes) * 2 + (1 - lanes % 2) == 2 * c + side, edge_values[c][side], values)
    values = jnp.where((lanes // 2 % planes == plane) & (lanes < 6 * planes), values, 0.0)
    chosen = (lax.broadcasted_iota(jnp.int32, (rows, slots), 0) == block % rows).astype(bf16)
    total = ye[...]
    for piece in reversed(split(values, 2)):
        total = total + jnp.dot(chosen, piece, preferred_element_type=f32)
    ye[...] = total


GROUP = 4


def place_lines(q, block, high_ref, low_ref, forcing, out):
    slots = high_ref.shape[0]
    rows, cols = forcing.shape[2:]
    step = GROUP * rows
    number = lax.broadcasted_iota(jnp.int32, (step, slots), 0) + q * step
    chosen = (number == block).astype(jnp.bfloat16)
    at = slice(q * GROUP, (q + 1) * GROUP)
    for c in range(3):
        lanes = slice(c * cols, (c + 1) * cols)
        total = jnp.dot(chosen, low_ref[:, lanes], preferred_element_type=jnp.float32)
        total = total + jnp.dot(chosen, high_ref[:, lanes], preferred_element_type=jnp.float32)
        total = total.reshape(GROUP, rows, cols)
        forcing[c, at] = total
        out[c, at] = out[c, at] + total


def pack_rows(fields, rows, cols, xe):
    for k, read in enumerate(fields):
        for h in range(2):
            half = slice(h * LANES, (h + 1) * LANES)
            xe[0, k : k + 1, half] = read(slice(0, 1), h)
            xe[1, k : k + 1, half] = read(slice(rows - 1, rows), h)


def pack_columns(fields, rows, ye):
    lanes = lane_iota()

    @pl.loop(0, rows // SUB)
    def _(r):
        at = pl.ds(pl.multiple_of(r * SUB, SUB), SUB)
        packed = jnp.zeros((SUB, LANES), jnp.float32)
        for k, read in fields:
            ends = jnp.where(lanes == 0, read(at, 0), read(at, 1))
            ends = pltpu.roll(ends, (2 * k + 1) % LANES, axis=1)
            packed = jnp.where(lanes // 2 == k, ends, packed)
        ye[at, :] = packed


def scaled_from(shape, axis, first, factor):
    return jnp.where(lax.broadcasted_iota(jnp.int32, shape, axis) < first, 1.0, factor)


def from_sides(below, above, index):
    inner = inside_flags(*index)
    odd = lane_iota(below.shape[0]) % 2 == 1
    below, above = below * inner[2], above * inner[3]
    moved = jnp.where(odd, pltpu.roll(below, 1, axis=1), pltpu.roll(above, LANES - 1, axis=1))
    return moved, jnp.where(odd, below, above)


def inside_flags(n_gx, n_gy):
    gx, gy = lax.axis_index("gx"), lax.axis_index("gy")
    flags = (gx > 0, gx < n_gx - 1, gy > 0, gy < n_gy - 1)
    return [flag.astype(jnp.float32) for flag in flags]


def shifted(rows, by):
    if isinstance(rows, slice):
        return slice(rows.start + by, rows.stop + by)
    return pl.ds(pl.multiple_of(rows.start + by, SUB), rows.size)


def clear_outside(planes, rows, cols, adj, uz, vv):
    zero = jnp.zeros((rows, cols), jnp.float32)
    for at in (0, planes + 1):
        uz[at] = zero
        for h in range(2):
            vv[at, h, PAD : PAD + rows, :] = zero[:, :LANES]
            for c in range(3):
                adj[c, at, h, PAD : PAD + rows, :] = zero[:, :LANES]


def set_fields(z, vel, visc, ux, uy, uz, vv):
    rows = visc.shape[1]
    if uy is not None:
        uy[z + 1] = vel[1, z].astype(jnp.float32) * half_step
    uz[z + 1] = vel[2, z].astype(jnp.float32) * half_step
    for h in range(2):
        half = slice(h * LANES, (h + 1) * LANES)
        vv[z + 1, h, PAD : PAD + rows, :] = visc[z, :, half].astype(jnp.float32) * half_step
        ux[z + 1, h, PAD : PAD + rows, :] = vel[0, z, :, half].astype(jnp.float32) * half_step


def clear_rows(planes, rows, adj, ux, vv):
    zero = jnp.zeros((PAD, LANES), jnp.float32)
    for at in (0, PAD + rows):
        for z in range(planes):
            for h in range(2):
                for ref in (ux, vv):
                    ref[z + 1, h, at : at + PAD, :] = zero
                for c in range(3):
                    adj[c, z + 1, h, at : at + PAD, :] = zero


def add_rows(planes, rows, xe, xh, out):
    for side, at, sign in ((0, 0, 1.0), (1, rows - 1, -1.0)):
        v_out = xh[side, 4 * planes : 5 * planes, :]
        coef = xe[side, 4 * planes : 5 * planes, :] + v_out + sign * xh[side, 3 * planes : 4 * planes, :]
        for c in range(3):
            mine = slice(c * planes, (c + 1) * planes)
            share = coef * xh[side, mine, :] - v_out * xe[side, mine, :]
            for z in range(planes):
                out[c, z, at : at + 1, :] = out[c, z, at : at + 1, :] + share[z : z + 1, :]


def column_fix(planes, own, outside, normal):
    lanes = lane_iota(own.shape[0])
    coef = own + outside + jnp.where(lanes % 2 == 1, normal, -normal)

    def spread(x):
        for_c = [pltpu.roll(x, LANES - 2 * planes * (3 - c), axis=1) for c in range(3)]
        return jnp.where(lanes < 2 * planes, for_c[0], jnp.where(lanes < 4 * planes, for_c[1], for_c[2]))

    share = spread(coef) * outside - spread(outside) * own
    return jnp.where(lanes < 6 * planes, share, 0.0)


def add_columns(q, planes, rows, fix, out):
    lanes = lane_iota()
    left, right = slice(0, LANES), slice(LANES, 2 * LANES)
    for r in range(rows // SUB):
        at = slice(r * SUB, (r + 1) * SUB)
        packed = fix[at, :]
        for c in range(3):
            for z in range(q * GROUP, (q + 1) * GROUP):
                moved = pltpu.roll(packed, LANES - 1 - 2 * (c * planes + z), axis=1)
                out[c, z, at, left] = out[c, z, at, left] + jnp.where(lanes == 0, moved, 0.0)
                out[c, z, at, right] = out[c, z, at, right] + jnp.where(lanes == LANES - 1, moved, 0.0)


def set_rows(planes, rows, xa, xh, adj, ux, vv):
    for side, at in ((0, PAD - 1), (1, PAD + rows)):
        for z in range(planes):
            for h in range(2):
                half = slice(h * LANES, (h + 1) * LANES)
                for c in range(3):
                    k = c * planes + z
                    adj[c, z + 1, h, at : at + 1, :] = xa[side, k : k + 1, half]
                k = 3 * planes + z
                ux[z + 1, h, at : at + 1, :] = xh[side, k : k + 1, half]
                k = 4 * planes + z
                vv[z + 1, h, at : at + 1, :] = xh[side, k : k + 1, half]


def up_down(pair, outer, first, last):
    left, right = pair
    left_up, right_up = (pltpu.roll(x, LANES - 1, axis=1) for x in pair)
    left_down, right_down = (pltpu.roll(x, 1, axis=1) for x in pair)
    up = (jnp.where(last, right_up, left_up), jnp.where(last, outer, right_up))
    down = (jnp.where(first, outer, left_down), jnp.where(first, left_down, right_down))
    return up, down


def sweep_plane(z, planes, rows, adj, ux, uz, vv, vel, visc, yhs, forcing, out):
    lanes = lane_iota()
    first, last = lanes == 0, lanes == LANES - 1
    here = z + 1
    both = (slice(0, LANES), slice(LANES, 2 * LANES))
    zero = jnp.zeros((SUB, LANES), jnp.float32)

    def outer(edges, k):
        return zero if edges is None else pltpu.roll(edges, LANES - 1 - 2 * (k * planes + z), axis=1)

    def turned(ref, index, pair_rows):
        out = []
        for half in both:
            x = ref[(*index, pair_rows, half)]
            up, down = pltpu.roll(x, LANES - 1, axis=1), pltpu.roll(x, 1, axis=1)
            out.append([y.astype(jnp.float32) * half_step for y in (up, down)])
        return out

    def joined(field, strip, outside):
        (left_up, left_down), (right_up, right_down) = (
            [y[strip * SUB : (strip + 1) * SUB] for y in half] for half in field
        )
        up = (jnp.where(last, right_up, left_up), jnp.where(last, outside, right_up))
        down = (jnp.where(first, outside, left_down), jnp.where(first, left_down, right_down))
        return up, down

    for r in range(rows // SUB):
        at = slice(r * SUB, (r + 1) * SUB)
        mid, plus, minus = (slice(at.start + PAD + d, at.stop + PAD + d) for d in (0, 1, -1))
        edges = (None, None) if yhs is None else (yhs[0, at, :], yhs[1, at, :])
        if r % 2 == 0:
            pair_rows = slice(r * SUB, (r + 2) * SUB)
            v_turned, u_turned = turned(visc, (z,), pair_rows), turned(vel, (1, z), pair_rows)
        v = [vv[here, h, mid, :] for h in range(2)]
        v_yp, v_ym = joined(v_turned, r % 2, outer(edges[0], 3))
        u_yp, u_ym = joined(u_turned, r % 2, outer(edges[1], 3))
        coef = []
        for h in range(2):
            n_xp, n_xm = v[h] + vv[here, h, plus, :], v[h] + vv[here, h, minus, :]
            n_yp, n_ym = v[h] + v_yp[h], v[h] + v_ym[h]
            n_zp, n_zm = v[h] + vv[here + 1, h, mid, :], v[h] + vv[here - 1, h, mid, :]
            coef.append(
                (
                    1.0 - ((n_xp + n_xm) + (n_yp + n_ym) + (n_zp + n_zm)),
                    n_xp - ux[here, h, plus, :],
                    n_xm + ux[here, h, minus, :],
                    n_yp - u_yp[h],
                    n_ym + u_ym[h],
                    n_zp - uz[here + 1, at, both[h]],
                    n_zm + uz[here - 1, at, both[h]],
                )
            )
        for c in range(3):
            a = [adj[c, here, h, mid, :] for h in range(2)]
            a_yp, a_ym = up_down(a, outer(edges[0], c), first, last)
            for h in range(2):
                k = coef[h]
                value = k[0] * a[h] + (k[1] * adj[c, here, h, plus, :] + k[2] * adj[c, here, h, minus, :])
                value = value + (k[3] * a_yp[h] + k[4] * a_ym[h])
                value = value + (k[5] * adj[c, here + 1, h, mid, :] + k[6] * adj[c, here - 1, h, mid, :])
                if forcing is not None:
                    value = value + forcing[c, z, at, both[h]]
                out[c, z, at, both[h]] = value


def first_kernel(n_gx, n_gy, *refs):
    (source, block, count, weight, obs_in, weights_in, vel_in, ke_in, dr_in, adj_in,
     out_hbm, f_hbm, visc_hbm, xh_hbm, yc_hbm, xa, ya,
     slots, recv, obs, weights, vel, ke, dr, visc, adj, ux, uy, uz, vv, yhs, out, frc, high, low, xe, xh, ye, xe2, ye2, yfix,
     x_out, x_in, y_out, y_in, x_out2, y_out2,
     load, save, all_send, all_recv, local_sem, send, received) = refs
    planes, rows, cols = visc.shape
    peers = n_gx * n_gy
    gx, gy = lax.axis_index("gx"), lax.axis_index("gy")
    me = gx * n_gy + gy

    def device(step):
        peer = lax.rem(me + step, peers)
        return peer, (peer // n_gy, lax.rem(peer, n_gy))

    lower_x = (lax.rem(gx + n_gx - 1, n_gx), gy)
    upper_x = (lax.rem(gx + 1, n_gx), gy)
    lower_y = (gx, lax.rem(gy + n_gy - 1, n_gy))
    upper_y = (gx, lax.rem(gy + 1, n_gy))

    def edge_copies(turn, x_from, y_from, x_to, y_to):
        sides = (
            (x_from.at[1], x_to.at[0], upper_x),
            (x_from.at[0], x_to.at[1], lower_x),
            (y_from[1], y_to.at[0], upper_y),
            (y_from[0], y_to.at[1], lower_y),
        )
        return [
            pltpu.make_async_remote_copy(
                here, there, send.at[turn, k], received.at[turn, k], device_id=where, device_id_type=MESH
            )
            for k, (here, there, where) in enumerate(sides)
        ]

    loads = [
        pltpu.make_async_copy(ke_in, ke, load.at[0]),
        pltpu.make_async_copy(dr_in, dr, load.at[1]),
        pltpu.make_async_copy(vel_in, vel, load.at[2]),
    ] + [
        pltpu.make_async_copy(
            adj_in.at[:, :, :, pl.ds(h * LANES, LANES)],
            adj.at[:, pl.ds(1, planes), h, pl.ds(PAD, rows), :],
            load.at[3 + h],
        )
        for h in range(2)
    ]
    ahead = [
        pltpu.make_async_copy(obs_in, obs, load.at[5]),
        pltpu.make_async_copy(weights_in, weights, load.at[6]),
    ]
    for copy in ahead + loads:
        copy.start()
    barrier = pltpu.get_barrier_semaphore()

    @pl.loop(1, peers)
    def _(step):
        pl.semaphore_signal(barrier, inc=1, device_id=device(step)[1], device_id_type=MESH)

    for copy in ahead:
        copy.wait()
    fill_slots(source[...], block[...], count[...], weight[...], obs, slots, rows)
    clear_outside(planes, rows, cols, adj, uz, vv)
    for copy in loads[:3]:
        copy.wait()

    @pl.loop(0, planes)
    def _(z):
        value = base_viscosity + ke[z].astype(jnp.float32) / dr[z].astype(jnp.float32)
        visc[z] = value.astype(jnp.bfloat16)
        set_fields(z, vel, visc, ux, uy, uz, vv)

    visc_save = pltpu.make_async_copy(visc, visc_hbm, save.at[8])
    visc_save.start()
    for copy in loads[3:]:
        copy.wait()

    def of_adj(c, z):
        return lambda at, h: adj[c, z + 1, h, shifted(at, PAD), :]

    def of_tall(ref, z):
        return lambda at, h: ref[z + 1, h, shifted(at, PAD), :]

    def of_uy(z):
        return lambda at, h: uy[z + 1, at, slice(h * LANES, (h + 1) * LANES)]

    starts = [of_adj(c, z) for c in range(3) for z in range(planes)]
    visc_fields = [of_tall(vv, z) for z in range(planes)]
    pack_rows(starts + [of_tall(ux, z) for z in range(planes)] + visc_fields, rows, cols, xe)
    pack_columns(list(enumerate(starts + visc_fields)), rows, ye.at[0])
    pack_columns([(3 * planes + z, of_uy(z)) for z in range(planes)], rows, ye.at[1])

    bf16, f32 = jnp.bfloat16, jnp.float32
    unscale_rows = scaled_from(xe.shape[1:], 0, 3 * planes, 1.0 / half_step)
    unscale_lanes = scaled_from((rows, LANES), 1, 6 * planes, 1.0 / half_step)
    for side in range(2):
        x_out[side] = (xe[side] * unscale_rows).astype(bf16)
    odd = lane_iota(rows) % 2 == 1
    main, normal = ye[0] * unscale_lanes, ye[1] * unscale_lanes
    y_out[0] = jnp.where(odd, main, pltpu.roll(normal, LANES - 1, axis=1)).astype(bf16)
    y_out[1] = jnp.where(odd, pltpu.roll(normal, 1, axis=1), main).astype(bf16)

    pl.semaphore_wait(barrier, peers - 1)
    copies = edge_copies(0, x_out, (y_out.at[0], y_out.at[1]), x_in, y_in)
    for copy in copies:
        copy.start()
    own = pltpu.make_async_copy(slots.at[me], recv.at[me], local_sem)
    own.start()

    def send_slots(step):
        peer, where = device(step)
        pltpu.make_async_remote_copy(
            slots.at[peer], recv.at[me], all_send, all_recv, device_id=where, device_id_type=MESH
        ).start()

    pl.loop(1, peers)(send_slots)

    clear_rows(planes, rows, adj, ux, vv)

    @pl.loop(0, planes)
    def _(z):
        sweep_plane(z, planes, rows, adj, ux, uz, vv, vel, visc, None, None, out)

    for copy in copies:
        copy.wait()
    index = (n_gx, n_gy)
    inner = inside_flags(*index)
    scale_rows = scaled_from(xe.shape[1:], 0, 3 * planes, half_step)
    scale_lanes = scaled_from((rows, LANES), 1, 6 * planes, half_step)
    for side in range(2):
        xh[side] = x_in[side].astype(f32) * (scale_rows * inner[side])
    below, above = (y_in[side].astype(f32) * scale_lanes for side in range(2))
    yhs[0], yhs[1] = from_sides(below, above, index)
    side_saves = [
        pltpu.make_async_copy(xh, xh_hbm, save.at[9]),
        pltpu.make_async_copy(yhs, yc_hbm, save.at[10]),
    ]
    for copy in side_saves:
        copy.start()
    add_rows(planes, rows, xe, xh, out)
    fix = column_fix(planes, ye[0], yhs[0], yhs[1])
    yfix[...] = fix

    def of_out(c, z):
        return lambda at, h: out[c, z, at, slice(h * LANES, (h + 1) * LANES)]

    news = [of_out(c, z) for c in range(3) for z in range(planes)]
    pack_rows(news, rows, cols, xe2)
    pack_columns(list(enumerate(news)), rows, ye2)
    ye2[...] = ye2[...] + fix
    for side, at in ((0, 0), (1, rows - 1)):
        row = jnp.broadcast_to(fix[at : at + 1], (3 * planes, LANES))
        spot = lax.broadcasted_iota(jnp.int32, row.shape, 1)
        field = 2 * lax.broadcasted_iota(jnp.int32, row.shape, 0)
        for which, lane, half in ((1, 0, slice(0, LANES)), (0, LANES - 1, slice(LANES, 2 * LANES))):
            corner = jnp.sum(jnp.where(spot == field + which, row, 0.0), axis=1, keepdims=True)
            xe2[side, :, half] = xe2[side, :, half] + jnp.where(spot == lane, corner, 0.0)

    own.wait()
    rest = pl.ds(0, peers - 1)
    pltpu.make_async_copy(slots.at[rest], slots.at[rest], all_send).wait()
    pltpu.make_async_copy(recv.at[rest], recv.at[rest], all_recv).wait()
    quarters = read_slots(recv)
    edge_values = line_forcing(quarters, vel, weights, high, low)
    across = quarters[3].T
    block = (across[PLANE : PLANE + 1] * rows + across[ROW : ROW + 1]).astype(jnp.int32)
    force_edges(block, quarters[3], edge_values, high, low, planes, rows, xe2, ye2)
    x_out2[...] = xe2[...].astype(bf16)
    y_out2[...] = ye2[...].astype(bf16)
    copies = edge_copies(1, x_out2, (y_out2, y_out2), xa, ya)
    for copy in copies:
        copy.start()
    saves = []
    for q in range(planes // GROUP):
        add_columns(q, planes, rows, yfix, out)
        place_lines(q, block, high, low, frc, out)
        at = pl.ds(q * GROUP, GROUP)
        saves.append(pltpu.make_async_copy(frc.at[:, at], f_hbm.at[:, at], save.at[2 * q]))
        saves.append(pltpu.make_async_copy(out.at[:, at], out_hbm.at[:, at], save.at[2 * q + 1]))
        for copy in saves[-2:]:
            copy.start()
    for copy in copies + saves + side_saves:
        copy.wait()
    visc_save.wait()


def second_kernel(n_gx, n_gy, starts, *refs):
    (f_in, vel_in, visc_in, adj_in, xh_in, yc_in, xa_in, ya_in,
     out_hbm,
     vel, visc, adj, ux, uy, uz, vv, yhs, out, frc, xh, yc, x_in, y_in, xa, load, save) = refs
    planes, rows, cols = visc.shape
    ends = starts[1:] + (planes,)

    def group(g):
        here = pl.ds(starts[g], ends[g] - starts[g])
        there = pl.ds(starts[g] + 1, ends[g] - starts[g])
        return [
            pltpu.make_async_copy(vel_in.at[:, here], vel.at[:, here], load.at[0, g]),
            pltpu.make_async_copy(visc_in.at[here], visc.at[here], load.at[1, g]),
            pltpu.make_async_copy(f_in.at[:, here], frc.at[:, here], load.at[2, g]),
        ] + [
            pltpu.make_async_copy(
                adj_in.at[:, here, :, pl.ds(h * LANES, LANES)],
                adj.at[:, there, h, pl.ds(PAD, rows), :],
                load.at[3 + h, g],
            )
            for h in range(2)
        ]

    groups = [group(g) for g in range(len(starts))]
    sides = [
        pltpu.make_async_copy(a, b, load.at[5, k])
        for k, (a, b) in enumerate(((xh_in, xh), (xa_in, x_in), (yc_in, yc), (ya_in, y_in)))
    ]
    for copies in [sides] + groups:
        for copy in copies:
            copy.start()
    clear_outside(planes, rows, cols, adj, uz, vv)
    for copy in sides:
        copy.wait()
    index = (n_gx, n_gy)
    inner = inside_flags(*index)
    for side in range(2):
        xa[side] = x_in[side].astype(jnp.float32) * inner[side]
    set_rows(planes, rows, xa, xh, adj, ux, vv)
    below, above = (y_in[side].astype(jnp.float32) for side in range(2))
    adjoint_lanes = lane_iota(rows) < 6 * planes
    yhs[0] = jnp.where(adjoint_lanes, from_sides(below, above, index)[0], yc[0])
    yhs[1] = yc[1]

    def fields(z):
        set_fields(z, vel, visc, ux, None, uz, vv)

    for copy in groups[0]:
        copy.wait()
    fields(0)

    @pl.loop(0, planes)
    def _(z):
        for g in range(1, len(starts)):

            @pl.when(z + 1 == starts[g])
            def _():
                for copy in groups[g]:
                    copy.wait()

        @pl.when(z + 1 < planes)
        def _():
            fields(z + 1)

        sweep_plane(z, planes, rows, adj, ux, uz, vv, vel, visc, yhs, frc, out)
        pltpu.make_async_copy(out.at[:, z], out_hbm.at[:, z], save).start()

    pltpu.make_async_copy(out, out_hbm, save).wait()


def field_scratch(planes, rows, cols):
    f32, bf16 = jnp.float32, jnp.bfloat16
    tall = rows + 2 * PAD
    return [
        pltpu.VMEM((planes, rows, cols), bf16),
        pltpu.VMEM((3, planes + 2, 2, tall, LANES), f32),
        pltpu.VMEM((planes + 2, 2, tall, LANES), f32),
        pltpu.VMEM((planes + 2, rows, cols), f32),
        pltpu.VMEM((planes + 2, rows, cols), f32),
        pltpu.VMEM((planes + 2, 2, tall, LANES), f32),
        pltpu.VMEM((2, rows, LANES), f32),
        pltpu.VMEM((3, planes, rows, cols), f32),
        pltpu.VMEM((3, planes, rows, cols), f32),
    ]


def local(
    n_gx,
    n_gy,
    velocity,
    kinetic_energy,
    dissipation_rate,
    adjoint_start,
    interp_weight,
    observed,
    window_weight,
    window_source,
    window_block,
    window_count,
):
    planes, rows, cols = kinetic_energy.shape
    peers = n_gx * n_gy
    windows = window_block.shape[0]
    f32, bf16 = jnp.float32, jnp.bfloat16
    shape = jax.ShapeDtypeStruct
    vmem = pl.BlockSpec(memory_space=pltpu.VMEM)
    hbm = pl.BlockSpec(memory_space=pl.ANY)
    dma = pltpu.SemaphoreType.DMA
    whole = shape(adjoint_start.shape, f32)
    sides = [
        shape((2, 5 * planes, cols), f32),
        shape((2, rows, LANES), f32),
        shape((2, 3 * planes, cols), bf16),
        shape((2, rows, LANES), bf16),
    ]
    edges = [
        (2, 5 * planes, cols),
        (2, 5 * planes, cols),
        (2, rows, LANES),
        (2, 3 * planes, cols),
        (rows, LANES),
        (rows, LANES),
    ]
    messages = [
        (2, 5 * planes, cols),
        (2, 5 * planes, cols),
        (2, rows, LANES),
        (2, rows, LANES),
        (2, 3 * planes, cols),
        (rows, LANES),
    ]
    flat = (1, windows)
    adjoint, forcing, visc, xh, yc, xa, ya = pl.pallas_call(
        functools.partial(first_kernel, n_gx, n_gy),
        name="route_and_first_sweep",
        in_specs=[vmem] * 4 + [hbm] * 6,
        out_specs=[hbm] * 7,
        out_shape=[whole, whole, shape((planes, rows, cols), bf16)] + sides,
        scratch_shapes=[
            pltpu.VMEM((peers, SUB, HALF), bf16),
            pltpu.VMEM((peers, SUB, HALF), bf16),
            pltpu.VMEM(observed.shape, f32),
            pltpu.VMEM(interp_weight.shape, bf16),
            pltpu.VMEM((3, planes, rows, cols), bf16),
            pltpu.VMEM((planes, rows, cols), bf16),
            pltpu.VMEM((planes, rows, cols), bf16),
        ]
        + field_scratch(planes, rows, cols)
        + [
            pltpu.VMEM((peers * CAP, 3 * cols), bf16),
            pltpu.VMEM((peers * CAP, 3 * cols), bf16),
        ]
        + [pltpu.VMEM(e, f32) for e in edges] + [pltpu.VMEM(e, bf16) for e in messages]
        + [dma((7,)), dma((2 * planes // GROUP + 3,)), dma, dma, dma, dma((2, 4)), dma((2, 4))],
        compiler_params=pltpu.CompilerParams(
            collective_id=0, has_side_effects=True, vmem_limit_bytes=60 << 20
        ),
    )(
        window_source.reshape(flat),
        window_block.reshape(flat),
        window_count.reshape(flat),
        window_weight.reshape(flat),
        observed,
        interp_weight,
        velocity,
        kinetic_energy,
        dissipation_rate,
        adjoint_start,
    )
    starts = (0, 1, 2, 4, 8, 12)
    return pl.pallas_call(
        functools.partial(second_kernel, n_gx, n_gy, starts),
        name="second_sweep",
        in_specs=[hbm] * 8,
        out_specs=hbm,
        out_shape=whole,
        scratch_shapes=[pltpu.VMEM((3, planes, rows, cols), bf16)]
        + field_scratch(planes, rows, cols)
        + [pltpu.VMEM(side.shape, side.dtype) for side in sides]
        + [pltpu.VMEM(sides[2].shape, f32)]
        + [dma((6, len(starts))), dma],
        compiler_params=pltpu.CompilerParams(vmem_limit_bytes=60 << 20),
    )(forcing, velocity, visc, adjoint, xh, yc, xa, ya)


def solution(mesh):
    placed = (
        P(None, None, "gx", "gy"),
        P(None, "gx", "gy"),
        P(None, "gx", "gy"),
        P(None, None, "gx", "gy"),
        P(),
        P(None, ("gx", "gy"), None),
        P(("gx", "gy")),
        P(("gx", "gy"), None),
        P(("gx", "gy")),
        P(("gx", "gy")),
    )
    return jax.shard_map(
        functools.partial(local, mesh.shape["gx"], mesh.shape["gy"]),
        mesh=mesh,
        in_specs=placed,
        out_specs=P(None, None, "gx", "gy"),
        check_vma=False,
    )
```

```python
import functools

import jax
import jax.numpy as jnp
from jax import lax
from jax.experimental import pallas as pl
from jax.experimental.pallas import tpu as pltpu
from jax.sharding import PartitionSpec as P

MESH = pl.DeviceIdType.MESH
SWEEPS = 2
CAP = 4
LANES = 128
SUB = 8

base_viscosity = 0.05
pseudo_step = 0.4
half_step = 0.5 * pseudo_step

HALF = 2 * LANES
PLANE, ROW, COUNT, WEIGHT = 0, 1, 2, 3
PAD = 8


def lane_iota(rows=SUB):
    return lax.broadcasted_iota(jnp.int32, (rows, LANES), 1)


def split(x, pieces):
    out = []
    for _ in range(pieces):
        piece = x.astype(jnp.bfloat16)
        out.append(piece)
        x = x - piece.astype(jnp.float32)
    return out


def fill_slots(source, block, count, weight, obs_ref, slots_ref, rows):
    windows = source.shape[1]
    peers = slots_ref.shape[0]
    slots = peers * CAP
    f32 = jnp.float32
    meta = [block // rows, block % rows, count] + split(weight, 3) + [source]
    meta = [row.astype(f32) for row in meta]
    meta = jnp.concatenate(meta + [jnp.zeros((LANES - len(meta), windows), f32)], axis=0).T
    first = lax.broadcasted_iota(jnp.int32, (windows, windows), 0)
    second = lax.broadcasted_iota(jnp.int32, (windows, windows), 1)
    same = (meta[:, 6:7] == source.astype(f32)) & (first < second)
    place = jnp.sum(same.astype(f32), axis=0, keepdims=True).astype(jnp.int32)
    chosen = lax.broadcasted_iota(jnp.int32, (slots, windows), 0) == source * CAP + place
    chosen = chosen.astype(jnp.bfloat16)
    top = lax.broadcasted_iota(jnp.int32, (slots // SUB, SUB, LANES), 1) < CAP
    quarters = []
    for values in (obs_ref[0], obs_ref[1], obs_ref[2], meta):
        total = jnp.dot(chosen, values.astype(jnp.bfloat16), preferred_element_type=f32)
        quarters.append(total.reshape(slots // SUB, SUB, LANES))
    for h in range(2):
        upper, lower = quarters[h], quarters[2 + h]
        even = jnp.where(top, upper, pltpu.roll(lower, CAP, axis=1))
        odd = jnp.where(top, pltpu.roll(upper, CAP, axis=1), lower)
        both = jnp.stack([even, odd], axis=1).reshape(peers, SUB, LANES)
        slots_ref[:, :, h * LANES : (h + 1) * LANES] = both.astype(jnp.bfloat16)


def read_slots(recv_ref):
    peers = recv_ref.shape[0]
    top = lax.broadcasted_iota(jnp.int32, (peers // 2, SUB, LANES), 1) < CAP
    quarters = [None] * 4
    for h in range(2):
        half = recv_ref[:, :, h * LANES : (h + 1) * LANES].astype(jnp.float32)
        pairs = half.reshape(peers // 2, 2, SUB, LANES)
        even, odd = pairs[:, 0], pairs[:, 1]
        upper = jnp.where(top, even, pltpu.roll(odd, CAP, axis=1))
        lower = jnp.where(top, pltpu.roll(even, CAP, axis=1), odd)
        quarters[h] = upper.reshape(peers * CAP, LANES)
        quarters[2 + h] = lower.reshape(peers * CAP, LANES)
    return quarters


def line_forcing(quarters, vel_ref, weight_ref, high_ref, low_ref):
    meta = quarters[3]
    slots = meta.shape[0]
    planes, rows, cols = vel_ref.shape[1:]
    weights = weight_ref[...]
    block = (meta[:, PLANE : PLANE + 1] * rows + meta[:, ROW : ROW + 1]).astype(jnp.int32)
    count = meta[:, COUNT : COUNT + 1].astype(jnp.int32)
    scale = sum(meta[:, WEIGHT + k : WEIGHT + k + 1] for k in (2, 1, 0))
    inside = lax.broadcasted_iota(jnp.int32, (slots, cols), 1) < count
    group = 4
    lines = [jnp.zeros((slots, cols), jnp.float32) for _ in range(3)]
    for q in range(planes // group):
        number = lax.broadcasted_iota(jnp.int32, (slots, group * rows), 1) + q * group * rows
        chosen = (number == block).astype(jnp.bfloat16)
        for c in range(3):
            some = vel_ref[c, q * group : (q + 1) * group].reshape(group * rows, cols)
            lines[c] = lines[c] + jnp.dot(chosen, some, preferred_element_type=jnp.float32)
    edge_values = []
    for c in range(3):
        masked = jnp.where(inside, lines[c], 0.0).astype(jnp.bfloat16)
        predicted = lax.dot_general(
            masked, weights, (((1,), (1,)), ((), ())), preferred_element_type=jnp.float32
        )
        high, low = split(scale * (predicted - quarters[c]), 2)
        placed = jnp.dot(low, weights, preferred_element_type=jnp.float32)
        placed = placed + jnp.dot(high, weights, preferred_element_type=jnp.float32)
        placed = jnp.where(inside, pseudo_step * placed, 0.0)
        edge_values.append((placed[:, 0:1], placed[:, cols - 1 : cols]))
        high, low = split(placed, 2)
        high_ref[:, c * cols : (c + 1) * cols] = high
        low_ref[:, c * cols : (c + 1) * cols] = low
    return edge_values


def force_edges(block, meta, edge_values, high_ref, low_ref, planes, rows, xe, ye):
    f32, bf16 = jnp.float32, jnp.bfloat16
    slots, width = high_ref.shape
    cols = width // 3
    number = lax.broadcasted_iota(jnp.int32, (2 * planes, slots), 0)
    line = number % planes * rows + number // planes * (rows - 1)
    chosen = (line == block).astype(bf16)
    total = jnp.dot(chosen, low_ref[...], preferred_element_type=f32)
    total = total + jnp.dot(chosen, high_ref[...], preferred_element_type=f32)
    for side in range(2):
        for c in range(3):
            at = slice(c * planes, (c + 1) * planes)
            xe[side, at, :] = xe[side, at, :] + total[side * planes : (side + 1) * planes, c * cols : (c + 1) * cols]
    lanes = lane_iota(slots)
    plane = meta[:, PLANE : PLANE + 1].astype(jnp.int32)
    values = jnp.zeros((slots, LANES), f32)
    for c in range(3):
        for side in range(2):
            values = jnp.where(lanes // (2 * planes) * 2 + (1 - lanes % 2) == 2 * c + side, edge_values[c][side], values)
    values = jnp.where((lanes // 2 % planes == plane) & (lanes < 6 * planes), values, 0.0)
    chosen = (lax.broadcasted_iota(jnp.int32, (rows, slots), 0) == block % rows).astype(bf16)
    total = ye[...]
    for piece in reversed(split(values, 2)):
        total = total + jnp.dot(chosen, piece, preferred_element_type=f32)
    ye[...] = total


GROUP = 4


def place_lines(q, block, high_ref, low_ref, forcing, out):
    slots = high_ref.shape[0]
    rows, cols = forcing.shape[2:]
    step = GROUP * rows
    number = lax.broadcasted_iota(jnp.int32, (step, slots), 0) + q * step
    chosen = (number == block).astype(jnp.bfloat16)
    at = slice(q * GROUP, (q + 1) * GROUP)
    for c in range(3):
        lanes = slice(c * cols, (c + 1) * cols)
        total = jnp.dot(chosen, low_ref[:, lanes], preferred_element_type=jnp.float32)
        total = total + jnp.dot(chosen, high_ref[:, lanes], preferred_element_type=jnp.float32)
        total = total.reshape(GROUP, rows, cols)
        forcing[c, at] = total
        out[c, at] = out[c, at] + total


def pack_rows(fields, rows, cols, xe):
    for k, read in enumerate(fields):
        for h in range(2):
            half = slice(h * LANES, (h + 1) * LANES)
            xe[0, k : k + 1, half] = read(slice(0, 1), h)
            xe[1, k : k + 1, half] = read(slice(rows - 1, rows), h)


def pack_columns(jobs, rows):
    lanes = lane_iota()
    strips = 4

    @pl.loop(0, rows // SUB // strips)
    def _(r):
        for i in range(strips):
            at = pl.ds(pl.multiple_of((r * strips + i) * SUB, SUB), SUB)
            for fields, ye in jobs:
                packed = jnp.zeros((SUB, LANES), jnp.float32)
                for k, read in fields:
                    ends = jnp.where(lanes == 0, read(at, 0), read(at, 1))
                    ends = pltpu.roll(ends, (2 * k + 1) % LANES, axis=1)
                    packed = jnp.where(lanes // 2 == k, ends, packed)
                ye[at, :] = packed


def scaled_from(shape, axis, first, factor):
    return jnp.where(lax.broadcasted_iota(jnp.int32, shape, axis) < first, 1.0, factor)


def from_sides(below, above, index):
    inner = inside_flags(*index)
    odd = lane_iota(below.shape[0]) % 2 == 1
    below, above = below * inner[2], above * inner[3]
    moved = jnp.where(odd, pltpu.roll(below, 1, axis=1), pltpu.roll(above, LANES - 1, axis=1))
    return moved, jnp.where(odd, below, above)


def inside_flags(n_gx, n_gy):
    gx, gy = lax.axis_index("gx"), lax.axis_index("gy")
    flags = (gx > 0, gx < n_gx - 1, gy > 0, gy < n_gy - 1)
    return [flag.astype(jnp.float32) for flag in flags]


def shifted(rows, by):
    if isinstance(rows, slice):
        return slice(rows.start + by, rows.stop + by)
    return pl.ds(pl.multiple_of(rows.start + by, SUB), rows.size)


def clear_outside(planes, rows, cols, adj, uz, vv):
    zero = jnp.zeros((rows, cols), jnp.float32)
    for at in (0, planes + 1):
        uz[at] = zero
        for h in range(2):
            vv[at, h, PAD : PAD + rows, :] = zero[:, :LANES]
            for c in range(3):
                adj[c, at, h, PAD : PAD + rows, :] = zero[:, :LANES]


def set_fields(z, vel, visc, ux, uy, uz, vv):
    rows = visc.shape[1]
    if uy is not None:
        uy[z + 1] = vel[1, z].astype(jnp.float32) * half_step
    uz[z + 1] = vel[2, z].astype(jnp.float32) * half_step
    for h in range(2):
        half = slice(h * LANES, (h + 1) * LANES)
        vv[z + 1, h, PAD : PAD + rows, :] = visc[z, :, half].astype(jnp.float32) * half_step
        ux[z + 1, h, PAD : PAD + rows, :] = vel[0, z, :, half].astype(jnp.float32) * half_step


def clear_rows(planes, rows, adj, ux, vv):
    zero = jnp.zeros((PAD, LANES), jnp.float32)
    for at in (0, PAD + rows):
        for z in range(planes):
            for h in range(2):
                for ref in (ux, vv):
                    ref[z + 1, h, at : at + PAD, :] = zero
                for c in range(3):
                    adj[c, z + 1, h, at : at + PAD, :] = zero


def add_rows(planes, rows, xe, xh, out):
    for side, at, sign in ((0, 0, 1.0), (1, rows - 1, -1.0)):
        v_out = xh[side, 4 * planes : 5 * planes, :]
        coef = xe[side, 4 * planes : 5 * planes, :] + v_out + sign * xh[side, 3 * planes : 4 * planes, :]
        for c in range(3):
            mine = slice(c * planes, (c + 1) * planes)
            share = coef * xh[side, mine, :] - v_out * xe[side, mine, :]
            for z in range(planes):
                out[c, z, at : at + 1, :] = out[c, z, at : at + 1, :] + share[z : z + 1, :]


def column_fix(planes, own, outside, normal):
    lanes = lane_iota(own.shape[0])
    coef = own + outside + jnp.where(lanes % 2 == 1, normal, -normal)

    def spread(x):
        for_c = [pltpu.roll(x, LANES - 2 * planes * (3 - c), axis=1) for c in range(3)]
        return jnp.where(lanes < 2 * planes, for_c[0], jnp.where(lanes < 4 * planes, for_c[1], for_c[2]))

    share = spread(coef) * outside - spread(outside) * own
    return jnp.where(lanes < 6 * planes, share, 0.0)


def add_columns(q, planes, rows, fix, out):
    lanes = lane_iota()
    left, right = slice(0, LANES), slice(LANES, 2 * LANES)
    for r in range(rows // SUB):
        at = slice(r * SUB, (r + 1) * SUB)
        packed = fix[at, :]
        for c in range(3):
            for z in range(q * GROUP, (q + 1) * GROUP):
                moved = pltpu.roll(packed, LANES - 1 - 2 * (c * planes + z), axis=1)
                out[c, z, at, left] = out[c, z, at, left] + jnp.where(lanes == 0, moved, 0.0)
                out[c, z, at, right] = out[c, z, at, right] + jnp.where(lanes == LANES - 1, moved, 0.0)


def set_rows(planes, rows, xa, xh, adj, ux, vv):
    for side, at in ((0, PAD - 1), (1, PAD + rows)):
        for z in range(planes):
            for h in range(2):
                half = slice(h * LANES, (h + 1) * LANES)
                for c in range(3):
                    k = c * planes + z
                    adj[c, z + 1, h, at : at + 1, :] = xa[side, k : k + 1, half]
                k = 3 * planes + z
                ux[z + 1, h, at : at + 1, :] = xh[side, k : k + 1, half]
                k = 4 * planes + z
                vv[z + 1, h, at : at + 1, :] = xh[side, k : k + 1, half]


def up_down(pair, outer, first, last):
    left, right = pair
    left_up, right_up = (pltpu.roll(x, LANES - 1, axis=1) for x in pair)
    left_down, right_down = (pltpu.roll(x, 1, axis=1) for x in pair)
    up = (jnp.where(last, right_up, left_up), jnp.where(last, outer, right_up))
    down = (jnp.where(first, outer, left_down), jnp.where(first, left_down, right_down))
    return up, down


def sweep_plane(z, planes, rows, adj, ux, uz, vv, vel, visc, yhs, forcing, out):
    lanes = lane_iota()
    first, last = lanes == 0, lanes == LANES - 1
    here = z + 1
    both = (slice(0, LANES), slice(LANES, 2 * LANES))
    zero = jnp.zeros((SUB, LANES), jnp.float32)

    def outer(edges, k):
        return zero if edges is None else pltpu.roll(edges, LANES - 1 - 2 * (k * planes + z), axis=1)

    def turned(ref, index, pair_rows):
        out = []
        for half in both:
            x = ref[(*index, pair_rows, half)]
            up, down = pltpu.roll(x, LANES - 1, axis=1), pltpu.roll(x, 1, axis=1)
            out.append([y.astype(jnp.float32) * half_step for y in (up, down)])
        return out

    def joined(field, strip, outside):
        (left_up, left_down), (right_up, right_down) = (
            [y[strip * SUB : (strip + 1) * SUB] for y in half] for half in field
        )
        up = (jnp.where(last, right_up, left_up), jnp.where(last, outside, right_up))
        down = (jnp.where(first, outside, left_down), jnp.where(first, left_down, right_down))
        return up, down

    for r in range(rows // SUB):
        at = slice(r * SUB, (r + 1) * SUB)
        mid, plus, minus = (slice(at.start + PAD + d, at.stop + PAD + d) for d in (0, 1, -1))
        edges = (None, None) if yhs is None else (yhs[0, at, :], yhs[1, at, :])
        if r % 2 == 0:
            pair_rows = slice(r * SUB, (r + 2) * SUB)
            v_turned, u_turned = turned(visc, (z,), pair_rows), turned(vel, (1, z), pair_rows)
        v = [vv[here, h, mid, :] for h in range(2)]
        v_yp, v_ym = joined(v_turned, r % 2, outer(edges[0], 3))
        u_yp, u_ym = joined(u_turned, r % 2, outer(edges[1], 3))
        coef = []
        for h in range(2):
            n_xp, n_xm = v[h] + vv[here, h, plus, :], v[h] + vv[here, h, minus, :]
            n_yp, n_ym = v[h] + v_yp[h], v[h] + v_ym[h]
            n_zp, n_zm = v[h] + vv[here + 1, h, mid, :], v[h] + vv[here - 1, h, mid, :]
            coef.append(
                (
                    1.0 - ((n_xp + n_xm) + (n_yp + n_ym) + (n_zp + n_zm)),
                    n_xp - ux[here, h, plus, :],
                    n_xm + ux[here, h, minus, :],
                    n_yp - u_yp[h],
                    n_ym + u_ym[h],
                    n_zp - uz[here + 1, at, both[h]],
                    n_zm + uz[here - 1, at, both[h]],
                )
            )
        for c in range(3):
            a = [adj[c, here, h, mid, :] for h in range(2)]
            a_yp, a_ym = up_down(a, outer(edges[0], c), first, last)
            for h in range(2):
                k = coef[h]
                value = k[0] * a[h] + (k[1] * adj[c, here, h, plus, :] + k[2] * adj[c, here, h, minus, :])
                value = value + (k[3] * a_yp[h] + k[4] * a_ym[h])
                value = value + (k[5] * adj[c, here + 1, h, mid, :] + k[6] * adj[c, here - 1, h, mid, :])
                if forcing is not None:
                    value = value + forcing[c, z, at, both[h]]
                out[c, z, at, both[h]] = value


def first_kernel(n_gx, n_gy, *refs):
    (source, block, count, weight, obs_in, weights_in, vel_in, ke_in, dr_in, adj_in,
     out_hbm, f_hbm, visc_hbm, xh_hbm, yc_hbm, xa, ya,
     slots, recv, obs, weights, vel, ke, dr, visc, adj, ux, uy, uz, vv, yhs, out, frc, high, low, xe, xh, ye, xe2, ye2, yfix,
     x_out, x_in, y_out, y_in, x_out2, y_out2,
     load, save, all_send, all_recv, local_sem, send, received) = refs
    planes, rows, cols = visc.shape
    peers = n_gx * n_gy
    gx, gy = lax.axis_index("gx"), lax.axis_index("gy")
    me = gx * n_gy + gy

    def device(step):
        peer = lax.rem(me + step, peers)
        return peer, (peer // n_gy, lax.rem(peer, n_gy))

    lower_x = (lax.rem(gx + n_gx - 1, n_gx), gy)
    upper_x = (lax.rem(gx + 1, n_gx), gy)
    lower_y = (gx, lax.rem(gy + n_gy - 1, n_gy))
    upper_y = (gx, lax.rem(gy + 1, n_gy))

    def edge_copies(turn, x_from, y_from, x_to, y_to):
        sides = (
            (x_from.at[1], x_to.at[0], upper_x),
            (x_from.at[0], x_to.at[1], lower_x),
            (y_from[1], y_to.at[0], upper_y),
            (y_from[0], y_to.at[1], lower_y),
        )
        return [
            pltpu.make_async_remote_copy(
                here, there, send.at[turn, k], received.at[turn, k], device_id=where, device_id_type=MESH
            )
            for k, (here, there, where) in enumerate(sides)
        ]

    loads = [
        pltpu.make_async_copy(ke_in, ke, load.at[0]),
        pltpu.make_async_copy(dr_in, dr, load.at[1]),
        pltpu.make_async_copy(vel_in, vel, load.at[2]),
    ] + [
        pltpu.make_async_copy(
            adj_in.at[:, :, :, pl.ds(h * LANES, LANES)],
            adj.at[:, pl.ds(1, planes), h, pl.ds(PAD, rows), :],
            load.at[3 + h],
        )
        for h in range(2)
    ]
    ahead = [
        pltpu.make_async_copy(obs_in, obs, load.at[5]),
        pltpu.make_async_copy(weights_in, weights, load.at[6]),
    ]
    for copy in ahead + loads:
        copy.start()
    barrier = pltpu.get_barrier_semaphore()

    @pl.loop(1, peers)
    def _(step):
        pl.semaphore_signal(barrier, inc=1, device_id=device(step)[1], device_id_type=MESH)

    for copy in ahead:
        copy.wait()
    fill_slots(source[...], block[...], count[...], weight[...], obs, slots, rows)
    clear_outside(planes, rows, cols, adj, uz, vv)
    for copy in loads[:3]:
        copy.wait()

    @pl.loop(0, planes)
    def _(z):
        value = base_viscosity + ke[z].astype(jnp.float32) / dr[z].astype(jnp.float32)
        visc[z] = value.astype(jnp.bfloat16)
        set_fields(z, vel, visc, ux, uy, uz, vv)

    visc_save = pltpu.make_async_copy(visc, visc_hbm, save.at[8])
    visc_save.start()
    for copy in loads[3:]:
        copy.wait()

    def of_adj(c, z):
        return lambda at, h: adj[c, z + 1, h, shifted(at, PAD), :]

    def of_tall(ref, z):
        return lambda at, h: ref[z + 1, h, shifted(at, PAD), :]

    def of_uy(z):
        return lambda at, h: uy[z + 1, at, slice(h * LANES, (h + 1) * LANES)]

    starts = [of_adj(c, z) for c in range(3) for z in range(planes)]
    visc_fields = [of_tall(vv, z) for z in range(planes)]
    pack_rows(starts + [of_tall(ux, z) for z in range(planes)] + visc_fields, rows, cols, xe)
    normals = [(3 * planes + z, of_uy(z)) for z in range(planes)]
    pack_columns([(list(enumerate(starts + visc_fields)), ye.at[0]), (normals, ye.at[1])], rows)

    bf16, f32 = jnp.bfloat16, jnp.float32
    unscale_rows = scaled_from(xe.shape[1:], 0, 3 * planes, 1.0 / half_step)
    unscale_lanes = scaled_from((rows, LANES), 1, 6 * planes, 1.0 / half_step)
    for side in range(2):
        x_out[side] = (xe[side] * unscale_rows).astype(bf16)
    odd = lane_iota(rows) % 2 == 1
    main, normal = ye[0] * unscale_lanes, ye[1] * unscale_lanes
    y_out[0] = jnp.where(odd, main, pltpu.roll(normal, LANES - 1, axis=1)).astype(bf16)
    y_out[1] = jnp.where(odd, pltpu.roll(normal, 1, axis=1), main).astype(bf16)

    pl.semaphore_wait(barrier, peers - 1)
    copies = edge_copies(0, x_out, (y_out.at[0], y_out.at[1]), x_in, y_in)
    for copy in copies:
        copy.start()
    own = pltpu.make_async_copy(slots.at[me], recv.at[me], local_sem)
    own.start()

    def send_slots(step):
        peer, where = device(step)
        pltpu.make_async_remote_copy(
            slots.at[peer], recv.at[me], all_send, all_recv, device_id=where, device_id_type=MESH
        ).start()

    pl.loop(1, peers)(send_slots)

    clear_rows(planes, rows, adj, ux, vv)

    @pl.loop(0, planes)
    def _(z):
        sweep_plane(z, planes, rows, adj, ux, uz, vv, vel, visc, None, None, out)

    for copy in copies:
        copy.wait()
    index = (n_gx, n_gy)
    inner = inside_flags(*index)
    scale_rows = scaled_from(xe.shape[1:], 0, 3 * planes, half_step)
    scale_lanes = scaled_from((rows, LANES), 1, 6 * planes, half_step)
    for side in range(2):
        xh[side] = x_in[side].astype(f32) * (scale_rows * inner[side])
    below, above = (y_in[side].astype(f32) * scale_lanes for side in range(2))
    yhs[0], yhs[1] = from_sides(below, above, index)
    side_saves = [
        pltpu.make_async_copy(xh, xh_hbm, save.at[9]),
        pltpu.make_async_copy(yhs, yc_hbm, save.at[10]),
    ]
    for copy in side_saves:
        copy.start()
    add_rows(planes, rows, xe, xh, out)
    fix = column_fix(planes, ye[0], yhs[0], yhs[1])
    yfix[...] = fix

    def of_out(c, z):
        return lambda at, h: out[c, z, at, slice(h * LANES, (h + 1) * LANES)]

    news = [of_out(c, z) for c in range(3) for z in range(planes)]
    pack_rows(news, rows, cols, xe2)
    pack_columns([(list(enumerate(news)), ye2)], rows)
    ye2[...] = ye2[...] + fix
    for side, at in ((0, 0), (1, rows - 1)):
        row = jnp.broadcast_to(fix[at : at + 1], (3 * planes, LANES))
        spot = lax.broadcasted_iota(jnp.int32, row.shape, 1)
        field = 2 * lax.broadcasted_iota(jnp.int32, row.shape, 0)
        for which, lane, half in ((1, 0, slice(0, LANES)), (0, LANES - 1, slice(LANES, 2 * LANES))):
            corner = jnp.sum(jnp.where(spot == field + which, row, 0.0), axis=1, keepdims=True)
            xe2[side, :, half] = xe2[side, :, half] + jnp.where(spot == lane, corner, 0.0)

    own.wait()
    rest = pl.ds(0, peers - 1)
    pltpu.make_async_copy(slots.at[rest], slots.at[rest], all_send).wait()
    pltpu.make_async_copy(recv.at[rest], recv.at[rest], all_recv).wait()
    quarters = read_slots(recv)
    edge_values = line_forcing(quarters, vel, weights, high, low)
    across = quarters[3].T
    block = (across[PLANE : PLANE + 1] * rows + across[ROW : ROW + 1]).astype(jnp.int32)
    force_edges(block, quarters[3], edge_values, high, low, planes, rows, xe2, ye2)
    x_out2[...] = xe2[...].astype(bf16)
    y_out2[...] = ye2[...].astype(bf16)
    copies = edge_copies(1, x_out2, (y_out2, y_out2), xa, ya)
    for copy in copies:
        copy.start()
    saves = []
    for q in range(planes // GROUP):
        add_columns(q, planes, rows, yfix, out)
        place_lines(q, block, high, low, frc, out)
        at = pl.ds(q * GROUP, GROUP)
        saves.append(pltpu.make_async_copy(frc.at[:, at], f_hbm.at[:, at], save.at[2 * q]))
        saves.append(pltpu.make_async_copy(out.at[:, at], out_hbm.at[:, at], save.at[2 * q + 1]))
        for copy in saves[-2:]:
            copy.start()
    for copy in copies + saves + side_saves:
        copy.wait()
    visc_save.wait()


def second_kernel(n_gx, n_gy, starts, *refs):
    (f_in, vel_in, visc_in, adj_in, xh_in, yc_in, xa_in, ya_in,
     out_hbm,
     vel, visc, adj, ux, uy, uz, vv, yhs, out, frc, xh, yc, x_in, y_in, xa, load, save) = refs
    planes, rows, cols = visc.shape
    ends = starts[1:] + (planes,)

    def group(g):
        here = pl.ds(starts[g], ends[g] - starts[g])
        there = pl.ds(starts[g] + 1, ends[g] - starts[g])
        return [
            pltpu.make_async_copy(vel_in.at[:, here], vel.at[:, here], load.at[0, g]),
            pltpu.make_async_copy(visc_in.at[here], visc.at[here], load.at[1, g]),
            pltpu.make_async_copy(f_in.at[:, here], frc.at[:, here], load.at[2, g]),
        ] + [
            pltpu.make_async_copy(
                adj_in.at[:, here, :, pl.ds(h * LANES, LANES)],
                adj.at[:, there, h, pl.ds(PAD, rows), :],
                load.at[3 + h, g],
            )
            for h in range(2)
        ]

    groups = [group(g) for g in range(len(starts))]
    sides = [
        pltpu.make_async_copy(a, b, load.at[5, k])
        for k, (a, b) in enumerate(((xh_in, xh), (xa_in, x_in), (yc_in, yc), (ya_in, y_in)))
    ]
    for copies in [sides] + groups:
        for copy in copies:
            copy.start()
    clear_outside(planes, rows, cols, adj, uz, vv)
    for copy in sides:
        copy.wait()
    index = (n_gx, n_gy)
    inner = inside_flags(*index)
    for side in range(2):
        xa[side] = x_in[side].astype(jnp.float32) * inner[side]
    set_rows(planes, rows, xa, xh, adj, ux, vv)
    below, above = (y_in[side].astype(jnp.float32) for side in range(2))
    adjoint_lanes = lane_iota(rows) < 6 * planes
    yhs[0] = jnp.where(adjoint_lanes, from_sides(below, above, index)[0], yc[0])
    yhs[1] = yc[1]

    def fields(z):
        set_fields(z, vel, visc, ux, None, uz, vv)

    for copy in groups[0]:
        copy.wait()
    fields(0)

    @pl.loop(0, planes)
    def _(z):
        for g in range(1, len(starts)):

            @pl.when(z + 1 == starts[g])
            def _():
                for copy in groups[g]:
                    copy.wait()

        fields(jnp.minimum(z + 1, planes - 1))
        sweep_plane(z, planes, rows, adj, ux, uz, vv, vel, visc, yhs, frc, out)
        pltpu.make_async_copy(out.at[:, z], out_hbm.at[:, z], save).start()

    pltpu.make_async_copy(out, out_hbm, save).wait()


def field_scratch(planes, rows, cols):
    f32, bf16 = jnp.float32, jnp.bfloat16
    tall = rows + 2 * PAD
    return [
        pltpu.VMEM((planes, rows, cols), bf16),
        pltpu.VMEM((3, planes + 2, 2, tall, LANES), f32),
        pltpu.VMEM((planes + 2, 2, tall, LANES), f32),
        pltpu.VMEM((planes + 2, rows, cols), f32),
        pltpu.VMEM((planes + 2, rows, cols), f32),
        pltpu.VMEM((planes + 2, 2, tall, LANES), f32),
        pltpu.VMEM((2, rows, LANES), f32),
        pltpu.VMEM((3, planes, rows, cols), f32),
        pltpu.VMEM((3, planes, rows, cols), f32),
    ]


def local(
    n_gx,
    n_gy,
    velocity,
    kinetic_energy,
    dissipation_rate,
    adjoint_start,
    interp_weight,
    observed,
    window_weight,
    window_source,
    window_block,
    window_count,
):
    planes, rows, cols = kinetic_energy.shape
    peers = n_gx * n_gy
    windows = window_block.shape[0]
    f32, bf16 = jnp.float32, jnp.bfloat16
    shape = jax.ShapeDtypeStruct
    vmem = pl.BlockSpec(memory_space=pltpu.VMEM)
    hbm = pl.BlockSpec(memory_space=pl.ANY)
    dma = pltpu.SemaphoreType.DMA
    whole = shape(adjoint_start.shape, f32)
    sides = [
        shape((2, 5 * planes, cols), f32),
        shape((2, rows, LANES), f32),
        shape((2, 3 * planes, cols), bf16),
        shape((2, rows, LANES), bf16),
    ]
    edges = [
        (2, 5 * planes, cols),
        (2, 5 * planes, cols),
        (2, rows, LANES),
        (2, 3 * planes, cols),
        (rows, LANES),
        (rows, LANES),
    ]
    messages = [
        (2, 5 * planes, cols),
        (2, 5 * planes, cols),
        (2, rows, LANES),
        (2, rows, LANES),
        (2, 3 * planes, cols),
        (rows, LANES),
    ]
    flat = (1, windows)
    adjoint, forcing, visc, xh, yc, xa, ya = pl.pallas_call(
        functools.partial(first_kernel, n_gx, n_gy),
        name="route_and_first_sweep",
        in_specs=[vmem] * 4 + [hbm] * 6,
        out_specs=[hbm] * 7,
        out_shape=[whole, whole, shape((planes, rows, cols), bf16)] + sides,
        scratch_shapes=[
            pltpu.VMEM((peers, SUB, HALF), bf16),
            pltpu.VMEM((peers, SUB, HALF), bf16),
            pltpu.VMEM(observed.shape, f32),
            pltpu.VMEM(interp_weight.shape, bf16),
            pltpu.VMEM((3, planes, rows, cols), bf16),
            pltpu.VMEM((planes, rows, cols), bf16),
            pltpu.VMEM((planes, rows, cols), bf16),
        ]
        + field_scratch(planes, rows, cols)
        + [
            pltpu.VMEM((peers * CAP, 3 * cols), bf16),
            pltpu.VMEM((peers * CAP, 3 * cols), bf16),
        ]
        + [pltpu.VMEM(e, f32) for e in edges] + [pltpu.VMEM(e, bf16) for e in messages]
        + [dma((7,)), dma((2 * planes // GROUP + 3,)), dma, dma, dma, dma((2, 4)), dma((2, 4))],
        compiler_params=pltpu.CompilerParams(
            collective_id=0, has_side_effects=True, vmem_limit_bytes=60 << 20
        ),
    )(
        window_source.reshape(flat),
        window_block.reshape(flat),
        window_count.reshape(flat),
        window_weight.reshape(flat),
        observed,
        interp_weight,
        velocity,
        kinetic_energy,
        dissipation_rate,
        adjoint_start,
    )
    starts = (0, 1, 2, 4, 8, 12)
    return pl.pallas_call(
        functools.partial(second_kernel, n_gx, n_gy, starts),
        name="second_sweep",
        in_specs=[hbm] * 8,
        out_specs=hbm,
        out_shape=whole,
        scratch_shapes=[pltpu.VMEM((3, planes, rows, cols), bf16)]
        + field_scratch(planes, rows, cols)
        + [pltpu.VMEM(side.shape, side.dtype) for side in sides]
        + [pltpu.VMEM(sides[2].shape, f32)]
        + [dma((6, len(starts))), dma],
        compiler_params=pltpu.CompilerParams(vmem_limit_bytes=60 << 20),
    )(forcing, velocity, visc, adjoint, xh, yc, xa, ya)


def solution(mesh):
    placed = (
        P(None, None, "gx", "gy"),
        P(None, "gx", "gy"),
        P(None, "gx", "gy"),
        P(None, None, "gx", "gy"),
        P(),
        P(None, ("gx", "gy"), None),
        P(("gx", "gy")),
        P(("gx", "gy"), None),
        P(("gx", "gy")),
        P(("gx", "gy")),
    )
    return jax.shard_map(
        functools.partial(local, mesh.shape["gx"], mesh.shape["gy"]),
        mesh=mesh,
        in_specs=placed,
        out_specs=P(None, None, "gx", "gy"),
        check_vma=False,
    )
```
